32 devices in a mesh: dp: 8 (over z, y), tensor: 4 (over x, core).
Axes of the slice: x: 2, y: 2, z: 4, core: 2. Of those that a mesh axis runs over, the one named last changes fastest.
Arguments:
- tokens: bfloat16 [16384, 768], P('dp'), may hold values from -6 to 6
- w_query: bfloat16 [768, 768], P(None, 'tensor'), may hold values from -0.3125 to 0.3125
- w_key: bfloat16 [768, 768], P(None, 'tensor'), may hold values from -0.21875 to 0.21875
- w_value: bfloat16 [768, 768], P(None, 'tensor'), may hold values from -0.21875 to 0.21875
- b_query: float32 [768], P('tensor'), may hold values from -3 to 3
- b_value: float32 [768], P('tensor'), may hold values from -3 to 3
- w_out: bfloat16 [768, 768], P('tensor'), may hold values from -0.875 to 0.875
- b_out: float32 [768], replicated, may hold values from -3 to 3
- gain_attn: float32 [768], replicated, may hold values from 0.5 to 1.5
- shift_attn: float32 [768], replicated, may hold values from -3 to 3
- w_up: bfloat16 [768, 3072], P(None, 'tensor'), may hold values from -0.21875 to 0.21875
- b_up: float32 [3072], P('tensor'), may hold values from -3 to 3
- w_down: bfloat16 [3072, 768], P('tensor'), may hold values from -0.109375 to 0.109375
- b_down: float32 [768], replicated, may hold values from -3 to 3
- gain_ffn: float32 [768], replicated, may hold values from 0.5 to 1.5
- shift_ffn: float32 [768], replicated, may hold values from -3 to 3
- starts: int32 [8, 2], P('dp'), may hold values from 0 to 1792, as said below
- grad_out: bfloat16 [16384, 768], P('dp'), may hold values from -6 to 6
Outputs:
- result: bfloat16 [16384, 768], P('dp')
- grad_tokens: float32 [16384, 768], P(('dp', 'tensor'))
- grad_w_query: float32 [768, 768], P(None, 'tensor')
- grad_w_key: float32 [768, 768], P(None, 'tensor')
- grad_w_value: float32 [768, 768], P(None, 'tensor')
- grad_b_query: float32 [768], P('tensor')
- grad_b_value: float32 [768], P('tensor')
- grad_w_out: float32 [768, 768], P('tensor')
- grad_b_out: float32 [768], replicated
- grad_gain_attn: float32 [768], replicated
- grad_shift_attn: float32 [768], replicated
- grad_w_up: float32 [768, 3072], P(None, 'tensor')
- grad_b_up: float32 [3072], P('tensor')
- grad_w_down: float32 [3072, 768], P('tensor')
- grad_b_down: float32 [768], replicated
- grad_gain_ffn: float32 [768], replicated
- grad_shift_ffn: float32 [768], replicated
The draws below stay inside these ranges and needn't reach their ends.
Inputs may be any that keep to these rules, and one draw needn't show every extreme that they name: In each sequence the starts rise, every piece of 256 tokens lies inside the sequence, and consecutive starts differ by 256 or more, so pieces never intersect.
All inputs are finite; a program needn't handle non-finite values.
Results may differ from the reference program's by a relative error of at most 0.02.
Values may be sent and summed in bfloat16 or wider, within the bound.
No kernel may reach another device: no remote copies, remote signals or barrier semaphores. Data moves between devices by JAX's collectives and lax.ppermute only.
A program may use at most 128 MiB of HBM per device.

```python
import jax
import jax.numpy as jnp
from jax import lax

D = 768
HEADS = 12
HEAD_DIM = 64
FF = 3072
SEQ_LEN = 2048
PIECE = 256
PICS = 2
SEQS = 8
TOKENS = 16384
N_TENSOR = 4


def draw_starts(key, part):
    spare_room = SEQ_LEN - PICS * PIECE
    low_end = -(spare_room // 2)
    sampled = jax.random.randint(key, (SEQS, PICS), low_end, spare_room + spare_room // 2 + 1)
    clipped = jnp.clip(sampled, 0, spare_room)
    ordered = jnp.sort(clipped, axis=-1)
    return (ordered + jnp.arange(PICS, dtype=jnp.int32)[None, :] * PIECE).astype(jnp.int32)


def steps_of(rng, shape, cuts, low, largest):
    factor_of, own = 1.0, jax.random.fold_in(rng, 6)
    for dim, parts in cuts:
        steps = jnp.exp(jax.random.uniform(jax.random.fold_in(own, dim), (parts,), jnp.float32, low / len(cuts), largest / len(cuts)))
        factor_of = factor_of * jnp.repeat(steps, shape[dim] // parts).reshape([-1 if axis == dim else 1 for axis in range(len(shape))])
    return factor_of


def bell_draw(stream_key, shape, scale, most, cuts=(), kind=jnp.bfloat16):
    drawn = jax.random.normal(stream_key, shape, jnp.float32) * scale
    if len(cuts) > 0:
        drawn = steps_of(stream_key, shape, cuts, -0.22, 0.18) * drawn
    return jnp.clip(drawn, min=-most, max=most).astype(kind)


def setup_inputs(seed: int = 0) -> dict:
    streams_of = jax.random.split(jax.random.key(seed), 19)
    tokens = bell_draw(streams_of[0], (TOKENS, D), 1.0, 6.0, ((0, 8),))
    w_query = bell_draw(streams_of[1], (D, D), (D // 2) ** -0.5, 0.3125, ((1, 4),))
    w_key = bell_draw(streams_of[2], (D, D), D ** -0.5, 0.21875, ((1, 4),))
    w_value = bell_draw(streams_of[3], (D, D), D ** -0.5, 0.21875, ((1, 4),))
    b_query = bell_draw(streams_of[4], (D,), 0.5, 3.0, ((0, 4),), jnp.float32)
    b_value = bell_draw(streams_of[5], (D,), 0.5, 3.0, ((0, 4),), jnp.float32)
    w_out = bell_draw(streams_of[6], (D, D), (D // 16) ** -0.5, 0.875, ((0, 4),))
    b_out = bell_draw(streams_of[7], (D,), 0.5, 3.0, (), jnp.float32)
    gain_attn = jnp.clip(1.0 + 0.1 * jax.random.normal(streams_of[8], (D,), jnp.float32), 0.5, 1.5)
    shift_attn = bell_draw(streams_of[9], (D,), 0.5, 3.0, (), jnp.float32)
    w_up = bell_draw(streams_of[10], (D, FF), D ** -0.5, 0.21875, ((1, 4),))
    b_up = bell_draw(streams_of[11], (FF,), 0.5, 3.0, ((0, 4),), jnp.float32)
    w_down = bell_draw(streams_of[12], (FF, D), FF ** -0.5, 0.109375, ((0, 4),))
    b_down = bell_draw(streams_of[13], (D,), 0.5, 3.0, (), jnp.float32)
    gain_ffn = jnp.clip(1.0 + 0.1 * jax.random.normal(streams_of[14], (D,), jnp.float32), 0.5, 1.5)
    shift_ffn = bell_draw(streams_of[15], (D,), 0.5, 3.0, (), jnp.float32)
    starts = draw_starts(jax.random.fold_in(streams_of[18], 71), 0)
    grad_out = bell_draw(streams_of[17], (TOKENS, D), 1.0, 6.0, ((0, 8),))
    return dict(tokens=tokens, w_query=w_query, w_key=w_key, w_value=w_value, b_query=b_query, b_value=b_value, w_out=w_out, b_out=b_out, gain_attn=gain_attn, shift_attn=shift_attn, w_up=w_up, b_up=b_up, w_down=w_down, b_down=b_down, gain_ffn=gain_ffn, shift_ffn=shift_ffn, starts=starts, grad_out=grad_out)


@jax.custom_vjp
def low(v):
    return lax.optimization_barrier(v.astype(jnp.bfloat16)).astype(jnp.float32)

@jax.custom_vjp
def low_back(v):
    return v

def low_keep(v):
    return (low(v), None)

def low_pass(kept, grad):
    return (grad,)

def back_keep(v):
    return (v, None)

def back_low(kept, grad):
    return (low(grad),)
low.defvjp(low_keep, low_pass)
low_back.defvjp(back_keep, back_low)
EPSILON = 1e-12
HIGH = lax.Precision.HIGHEST

def matmul(left, right):
    return jnp.dot(left, right, precision=HIGH, preferred_element_type=jnp.float32)

def layer_norm(values, gain, shift):
    center = lax.optimization_barrier(jnp.mean(values, axis=-1, keepdims=True))
    spread = values - center
    variance = lax.optimization_barrier(jnp.mean(spread * spread, axis=-1, keepdims=True))
    return spread * lax.rsqrt(variance + EPSILON) * gain + shift

def allowed_mask(start_row, row_ids, col_ids):
    allowed = col_ids[None, :] <= row_ids[:, None]
    for piece_id in range(start_row.shape[0]):
        begin = start_row[piece_id]
        inside_rows = (row_ids >= begin) & (row_ids < begin + PIECE)
        inside_cols = (col_ids >= begin) & (col_ids < begin + PIECE)
        allowed = allowed | inside_rows[:, None] & inside_cols[None, :]
    return allowed

def layer_one(inputs, start_row, params):
    w_query, w_key, w_value, b_query, b_value, w_out, b_out, gain_attn, shift_attn, w_up, b_up, w_down, b_down, gain_ffn, shift_ffn = params
    length = inputs.shape[0]
    query_heads = low_back(low(matmul(inputs, w_query) + b_query)).reshape(length, HEADS, HEAD_DIM)
    key_heads = low_back(low(matmul(inputs, w_key))).reshape(length, HEADS, HEAD_DIM)
    value_heads = low_back(low(matmul(inputs, w_value) + b_value)).reshape(length, HEADS, HEAD_DIM)
    scores = low_back(jnp.einsum('qhd,khd->hqk', query_heads, key_heads, precision=HIGH) * 0.125)
    positions = jnp.arange(length, dtype=jnp.int32)
    allowed = allowed_mask(start_row, positions, positions)
    scores = jnp.where(allowed[None], scores, -1e+30)
    attention = jax.nn.softmax(scores, axis=-1)
    mixed_heads = jnp.einsum('hqk,khd->qhd', low(attention), value_heads, precision=HIGH).reshape(length, D)
    mixed_heads = low_back(low(mixed_heads))
    group_cols = D // N_TENSOR
    attn_sum = jnp.zeros((length, D), jnp.float32)
    for member in range(N_TENSOR):
        lower_col = member * group_cols
        attn_sum = attn_sum + low(matmul(mixed_heads[:, lower_col:lower_col + group_cols], w_out[lower_col:lower_col + group_cols]))
    hidden = layer_norm(inputs + low_back(attn_sum) + b_out, gain_attn, shift_attn)
    pre_gelu = low_back(matmul(low(hidden), w_up) + b_up)
    activated = low(jax.nn.gelu(pre_gelu, approximate=False))
    unit_cols = FF // N_TENSOR
    ffn_sum = jnp.zeros((length, D), jnp.float32)
    for member in range(N_TENSOR):
        lower_col = member * unit_cols
        ffn_sum = ffn_sum + low(matmul(activated[:, lower_col:lower_col + unit_cols], w_down[lower_col:lower_col + unit_cols]))
    return layer_norm(hidden + low_back(ffn_sum) + b_down, gain_ffn, shift_ffn)

def reference(tokens, w_query, w_key, w_value, b_query, b_value, w_out, b_out, gain_attn, shift_attn, w_up, b_up, w_down, b_down, gain_ffn, shift_ffn, starts, grad_out):
    params = tuple((weight.astype(jnp.float32) for weight in (w_query, w_key, w_value, b_query, b_value, w_out, b_out, gain_attn, shift_attn, w_up, b_up, w_down, b_down, gain_ffn, shift_ffn)))
    inputs = tokens.astype(jnp.float32).reshape(SEQS, SEQ_LEN, D)
    cotangent = grad_out.astype(jnp.float32).reshape(SEQS, SEQ_LEN, D)

    def one_sequence(totals, item):
        seq_in, start_row, seq_grad = item
        outcome, pull = jax.vjp(lambda data, weights: layer_one(data, start_row, weights), seq_in, params)
        grad_in, grad_params = pull(seq_grad)
        totals = jax.tree.map(lambda left, right: left + right, totals, grad_params)
        return (totals, (outcome, grad_in))
    initial = jax.tree.map(jnp.zeros_like, params)
    totals, (outcome, grad_in) = lax.scan(one_sequence, initial, (inputs, starts, cotangent))
    return (outcome.reshape(TOKENS, D).astype(jnp.bfloat16), grad_in.reshape(TOKENS, D), totals[0], totals[1], totals[2], totals[3], totals[4], totals[5], totals[6], totals[7], totals[8], totals[9], totals[10], totals[11], totals[12], totals[13], totals[14])
```

```python
import functools
import jax, jax.numpy as jnp
from jax import lax
from jax.sharding import PartitionSpec as P
from jax.experimental import pallas as pl
from jax.experimental.pallas import tpu as pltpu
F32, BF16 = jnp.float32, jnp.bfloat16
HD = 64
NEG = -1e30

def nn(a, b):
    return lax.dot_general(a, b, (((1,), (0,)), ((), ())), preferred_element_type=F32)

def flip(x):
    return x.astype(F32).T.astype(BF16)

def spread_rows(t, heads):
    out = []
    zero = jnp.zeros((HD, t.shape[1]), t.dtype)
    for h in range(heads):
        out.append(jnp.concatenate([t[g * HD:(g + 1) * HD] if g == h else zero for g in range(heads)], axis=0))
    return out

def spread_cols(t, heads):
    lane = lax.broadcasted_iota(jnp.int32, t.shape, 1)
    return [jnp.where((lane >= h * HD) & (lane < (h + 1) * HD), t, jnp.zeros_like(t)) for h in range(heads)]

def attn_fwd_kernel(half, QB, KB, count_ref, q_ref, k_ref, v_ref, lim_ref, o_ref, o32_ref, lse_ref, vx, acc, mx):
    rows = q_ref.shape[0]
    heads = q_ref.shape[1] // HD
    length = k_ref.shape[0]
    EX = HD + 16
    def fill(b, c):
        sl = pl.ds(pl.multiple_of(b * 256, 256), 256)
        vt = flip(v_ref[sl, :])
        row = lax.broadcasted_iota(jnp.int32, (16, 256), 0)
        one = jnp.where(row == 0, 1.0, 0.0).astype(BF16)
        for h in range(heads):
            vx[h, :, sl] = jnp.concatenate([vt[h * HD:(h + 1) * HD], one], axis=0)
        return c
    lax.fori_loop(0, length // 256, fill, 0)
    def q_block(i, c):
        qs = pl.ds(pl.multiple_of(i * QB, QB), QB)
        qm = spread_rows(flip(q_ref[qs, :]), heads)
        lim = lim_ref[:, qs]
        acc[...] = jnp.zeros_like(acc)
        mx[...] = jnp.full_like(mx, NEG)
        def k_block(masked, j, c):
            ks = pl.ds(pl.multiple_of(j * KB, KB), KB)
            kk = k_ref[ks, :]
            if masked:
                ok = lax.broadcasted_iota(jnp.int32, (KB, QB), 0) + j * KB <= lim
            for h in range(heads):
                s = nn(kk, qm[h])
                if masked:
                    s = jnp.where(ok, s, NEG)
                old = mx[h]
                new = jnp.maximum(old, jnp.max(s, axis=0, keepdims=True))
                p = jnp.exp(s - new).astype(BF16)
                acc[h] = acc[h] * jnp.exp(old - new) + nn(vx[h, :, ks], p)
                mx[h] = new
            return c
        first = half * rows + i * QB
        n_full = (first + 1) // KB
        lax.fori_loop(0, n_full, functools.partial(k_block, False), 0)
        lax.fori_loop(n_full, count_ref[half * (rows // QB) + i], functools.partial(k_block, True), 0)
        for h in range(heads):
            a = acc[h]
            total = a[HD:HD + 1]
            o = a[:HD] / total
            o32_ref[h * HD:(h + 1) * HD, qs] = o
            o_ref[h * HD:(h + 1) * HD, qs] = o.astype(BF16)
            lse_ref[h:h + 1, qs] = mx[h] + jnp.log(total)
        return c
    lax.fori_loop(0, rows // QB, q_block, 0)

def attn_fwd(half, count, q, k, v, lim, QB=256, KB=512):
    length, cols = q.shape
    heads = cols // HD
    rows = length // 2
    full = pl.BlockSpec((length, cols), lambda i, c: (0, 0))
    return pl.pallas_call(
        functools.partial(attn_fwd_kernel, half, QB, KB),
        grid_spec=pltpu.PrefetchScalarGridSpec(
            num_scalar_prefetch=1, grid=(1,),
            in_specs=[pl.BlockSpec((rows, cols), lambda i, c: (half, 0)), full, full,
                      pl.BlockSpec((1, rows), lambda i, c: (0, half))],
            out_specs=[pl.BlockSpec((cols, rows), lambda i, c: (0, 0))] * 2 + [pl.BlockSpec((heads, rows), lambda i, c: (0, 0))],
            scratch_shapes=[pltpu.VMEM((heads, HD + 16, length), BF16), pltpu.VMEM((heads, HD + 16, QB), F32), pltpu.VMEM((heads, 1, QB), F32)]),
        out_shape=[jax.ShapeDtypeStruct((cols, rows), BF16), jax.ShapeDtypeStruct((cols, rows), F32), jax.ShapeDtypeStruct((heads, rows), F32)],
        name=f"attn_fwd_{half}",
        cost_estimate=pl.CostEstimate(flops=(1 + 2 * half) * 4 * rows * rows * cols, bytes_accessed=6 * length * cols, transcendentals=rows * rows * heads),
    )(count, q, k, v, lim)

def attn_bwd_kernel(half, first_call, QB, KB, count_ref, q_ref, k_ref, v_ref, lim_ref, lse_ref, o32_ref, g_ref, *rest):
    if first_call:
        dq_ref, dk_ref, dv_ref, kt, dqt = rest
    else:
        dk_in, dv_in, dq_ref, dk_ref, dv_ref, kt, dqt = rest
    rows = q_ref.shape[0]
    heads = q_ref.shape[1] // HD
    length = k_ref.shape[0]
    def fill(b, c):
        sl = pl.ds(pl.multiple_of(b * 256, 256), 256)
        kt[:, sl] = flip(k_ref[sl, :])
        return c
    lax.fori_loop(0, length // 256, fill, 0)
    if first_call:
        dk_ref[...] = jnp.zeros_like(dk_ref)
        dv_ref[...] = jnp.zeros_like(dv_ref)
    else:
        dk_ref[...] = dk_in[...]
        dv_ref[...] = dv_in[...]
    def q_block(i, c):
        qs = pl.ds(pl.multiple_of(i * QB, QB), QB)
        q = q_ref[qs, :]
        g = g_ref[qs, :]
        gt32 = g.astype(F32).T
        qm = spread_rows(flip(q), heads)
        gm = spread_rows(gt32.astype(BF16), heads)
        qc = spread_cols(q, heads)
        gc = spread_cols(g, heads)
        prod = gt32 * o32_ref[:, qs]
        delta = [jnp.sum(prod[h * HD:(h + 1) * HD], axis=0, keepdims=True) for h in range(heads)]
        lse = [lse_ref[h:h + 1, qs] for h in range(heads)]
        lim = lim_ref[:, qs]
        dqt[...] = jnp.zeros_like(dqt)
        def k_block(masked, j, c):
            ks = pl.ds(pl.multiple_of(j * KB, KB), KB)
            kk = k_ref[ks, :]
            vv = v_ref[ks, :]
            if masked:
                ok = lax.broadcasted_iota(jnp.int32, (KB, QB), 0) + j * KB <= lim
            dk = dk_ref[ks, :]
            dv = dv_ref[ks, :]
            for h in range(heads):
                s = nn(kk, qm[h])
                p = jnp.exp(s - lse[h])
                if masked:
                    p = jnp.where(ok, p, 0.0)
                dp = nn(vv, gm[h])
                ds = (p * (dp - delta[h])).astype(BF16)
                dv = dv + nn(p.astype(BF16), gc[h])
                dk = dk + nn(ds, qc[h])
                dqt[h * HD:(h + 1) * HD] += nn(kt[h * HD:(h + 1) * HD, ks], ds)
            dk_ref[ks, :] = dk
            dv_ref[ks, :] = dv
            return c
        first = half * rows + i * QB
        n_full = (first + 1) // KB
        lax.fori_loop(0, n_full, functools.partial(k_block, False), 0)
        lax.fori_loop(n_full, count_ref[half * (rows // QB) + i], functools.partial(k_block, True), 0)
        dq_ref[qs, :] = (dqt[...] * 0.125).T.astype(BF16)
        return c
    lax.fori_loop(0, rows // QB, q_block, 0)

def attn_bwd(half, count, q, k, v, lim, lse, o32, g, carry=None, QB=256, KB=256):
    length, cols = q.shape
    heads = cols // HD
    rows = length // 2
    full = pl.BlockSpec((length, cols), lambda i, c: (0, 0))
    part = pl.BlockSpec((rows, cols), lambda i, c: (half, 0))
    ins = [q, k, v, lim, lse, o32, g]
    in_specs = [part, full, full, pl.BlockSpec((1, rows), lambda i, c: (0, half)), pl.BlockSpec((heads, rows), lambda i, c: (0, 0)),
                pl.BlockSpec((cols, rows), lambda i, c: (0, 0)), pl.BlockSpec((rows, cols), lambda i, c: (0, 0))]
    if carry is not None:
        ins += list(carry)
        in_specs += [full, full]
    return pl.pallas_call(
        functools.partial(attn_bwd_kernel, half, carry is None, QB, KB),
        grid_spec=pltpu.PrefetchScalarGridSpec(
            num_scalar_prefetch=1, grid=(1,), in_specs=in_specs,
            out_specs=[pl.BlockSpec((rows, cols), lambda i, c: (0, 0)), full, full],
            scratch_shapes=[pltpu.VMEM((cols, length), BF16), pltpu.VMEM((cols, QB), F32)]),
        out_shape=[jax.ShapeDtypeStruct((rows, cols), BF16), jax.ShapeDtypeStruct((length, cols), F32), jax.ShapeDtypeStruct((length, cols), F32)],
        name=f"attn_bwd_{half}",
        cost_estimate=pl.CostEstimate(flops=(1 + 2 * half) * 10 * rows * rows * cols, bytes_accessed=20 * length * cols, transcendentals=rows * rows * heads),
    )(count, *ins)

def limits(starts_row, length):
    pos = jnp.arange(length, dtype=jnp.int32)
    lim = pos
    for p in range(starts_row.shape[0]):
        b = starts_row[p]
        lim = jnp.where((pos >= b) & (pos < b + 256), b + 255, lim)
    return lim
def counts(lim, QB, KB):
    return jnp.max(lim.reshape(-1, QB), axis=1) // KB + 1

EPSILON = 1e-12

def nt(a, b):
    return lax.dot_general(a, b, (((1,), (1,)), ((), ())), preferred_element_type=F32)

def tn(a, b):
    return lax.dot_general(a, b, (((0,), (0,)), ((), ())), preferred_element_type=F32)

def standardized(v):
    spread = v - jnp.mean(v, axis=-1, keepdims=True)
    inv = lax.rsqrt(jnp.mean(spread * spread, axis=-1, keepdims=True) + EPSILON)
    return spread * inv, inv

def norm_back(n, inv, c):
    return inv * (c - jnp.mean(c, axis=-1, keepdims=True) - n * jnp.mean(c * n, axis=-1, keepdims=True))

def gelu_pair(v):
    cdf = 0.5 * (1.0 + lax.erf(v * 0.7071067811865476))
    pdf = jnp.exp(v * v * -0.5) * 0.3989422804014327
    return v * cdf, cdf + v * pdf

def qkv_kernel(tok, wq, wk, wv, bq, bv, q, k, v):
    t = tok[...]
    q[...] = ((nn(t, wq[...]) + bq[...]) * 0.125).astype(BF16)
    k[...] = nn(t, wk[...]).astype(BF16)
    v[...] = (nn(t, wv[...]) + bv[...]).astype(BF16)

def whole(shape):
    return pl.BlockSpec(shape, lambda *a: (0,) * len(shape))

def rows_of(block, cols):
    return pl.BlockSpec((block, cols), lambda i, *a: (i, 0))

def project_qkv(tokens, wq, wk, wv, bq, bv, block=512):
    rows, d = tokens.shape
    cols = wq.shape[1]
    return pl.pallas_call(
        qkv_kernel, grid=(rows // block,),
        in_specs=[rows_of(block, d)] + [whole((d, cols))] * 3 + [whole((1, cols))] * 2,
        out_specs=[rows_of(block, cols)] * 3,
        out_shape=[jax.ShapeDtypeStruct((rows, cols), BF16)] * 3,
        name="project_qkv",
        cost_estimate=pl.CostEstimate(flops=6 * rows * d * cols, bytes_accessed=2 * rows * (d + 3 * cols), transcendentals=0),
    )(tokens, wq, wk, wv, bq[None], bv[None])

def out_kernel(own, other, w_own, w_other, out):
    out[...] = (tn(own[...], w_own[...]) + tn(other[...], w_other[...])).astype(BF16)

def out_project(own, other, w_own, w_other):
    cols, rows = own.shape
    d = w_own.shape[1]
    return pl.pallas_call(
        out_kernel, out_shape=jax.ShapeDtypeStruct((rows, d), BF16), name="out_project",
        cost_estimate=pl.CostEstimate(flops=4 * rows * d * cols, bytes_accessed=2 * rows * (d + 2 * cols), transcendentals=0),
    )(own, other, w_own, w_other)

def ffn_fwd_kernel(spot, tok, p_own, p_far, b_out, gain, shift, up_a, up_b, bu_a, bu_b, down_a, down_b,
                   pre, low, act, slope, part):
    x = tok[...].astype(F32) + (p_own[...].astype(F32) + p_far[...].astype(F32)) + b_out[...]
    pre[...] = x
    n, inv = standardized(x)
    h = (n * gain[...] + shift[...]).astype(BF16)
    low[...] = h
    d = x.shape[1]
    total = None
    for s, (wu, bu, wd) in enumerate(((up_a, bu_a, down_a), (up_b, bu_b, down_b))):
        width = wu.shape[1]
        a, da = gelu_pair(nn(h, wu[...]) + bu[...])
        a = a.astype(BF16)
        act[:, s * width:(s + 1) * width] = a
        slope[:, s * width:(s + 1) * width] = da.astype(BF16)
        y = nn(a, wd[...])
        total = y if total is None else total + y
    part[...] = total.astype(BF16)

def ffn_fwd(half, core, tokens, p_own, p_far, b_out, gain, shift, ups, bus, downs, block=256):
    rows, d = p_own.shape
    width = ups[0].shape[1]
    steps = rows // block
    vec = whole((1, d))
    return pl.pallas_call(
        ffn_fwd_kernel,
        grid_spec=pltpu.PrefetchScalarGridSpec(
            num_scalar_prefetch=1, grid=(steps,),
            in_specs=[pl.BlockSpec((block, d), lambda i, c: ((2 * half + c[0]) * steps + i, 0)), rows_of(block, d), rows_of(block, d), vec, vec, vec]
            + [whole((d, width))] * 2 + [whole((1, width))] * 2 + [whole((width, d))] * 2,
            out_specs=[rows_of(block, d)] * 2 + [rows_of(block, 2 * width)] * 2 + [rows_of(block, d)]),
        out_shape=[jax.ShapeDtypeStruct((rows, d), F32), jax.ShapeDtypeStruct((rows, d), BF16)]
        + [jax.ShapeDtypeStruct((rows, 2 * width), BF16)] * 2 + [jax.ShapeDtypeStruct((rows, d), BF16)],
        name=f"ffn_fwd_{half}",
        cost_estimate=pl.CostEstimate(flops=8 * rows * d * width, bytes_accessed=rows * (14 * d + 8 * width), transcendentals=4 * rows * width),
    )(core, tokens, p_own, p_far, b_out, gain, shift, *ups, *bus, *downs)

def col_sum(v):
    return jnp.sum(v, axis=0, keepdims=True)

def ffn_bwd_kernel(spot, pre, p_own, p_far, go, slope, vecs, up_a, up_b, down_a, down_b,
                   result, d_low, d_pre, d_up, part, sums, bup):
    gain, shift, b_down, gain2, shift2 = (vecs[r:r + 1] for r in range(5))
    n, inv = standardized(pre[...])
    x = n * gain + shift + (p_own[...].astype(F32) + p_far[...].astype(F32)) + b_down
    n, inv = standardized(x)
    result[...] = (n * gain2 + shift2).astype(BF16)
    g = go[...].astype(F32)
    dx = norm_back(n, inv, g * gain2)
    d_pre[...] = dx
    dl = dx.astype(BF16)
    d_low[...] = dl
    stack = jnp.concatenate([col_sum(g * n), col_sum(g), col_sum(dx), jnp.zeros((5, dx.shape[1]), F32)], axis=0)
    total = None
    bu = []
    for s, (wu, wd) in enumerate(((up_a, down_a), (up_b, down_b))):
        width = wu.shape[1]
        sl = slice(s * width, (s + 1) * width)
        du = (nt(dl, wd[...]) * slope[:, sl].astype(F32)).astype(BF16)
        d_up[:, sl] = du
        bu.append(col_sum(du.astype(F32)))
        y = nt(du, wu[...])
        total = y if total is None else total + y
    part[...] = total.astype(BF16)
    bu = jnp.concatenate(bu + [jnp.zeros((6, bu[0].shape[1]), F32)], axis=0)
    @pl.when(pl.program_id(0) == 0)
    def _():
        sums[...] = stack
        bup[...] = bu
    @pl.when(pl.program_id(0) > 0)
    def _():
        sums[...] += stack
        bup[...] += bu

def ffn_bwd(half, core, pre, p_own, p_far, grad_out, slope, vecs, ups, downs, block=256):
    rows, d = pre.shape
    width = ups[0].shape[1]
    steps = rows // block
    return pl.pallas_call(
        ffn_bwd_kernel,
        grid_spec=pltpu.PrefetchScalarGridSpec(
            num_scalar_prefetch=1, grid=(steps,),
            in_specs=[rows_of(block, d)] * 3 + [pl.BlockSpec((block, d), lambda i, c: ((2 * half + c[0]) * steps + i, 0)), rows_of(block, 2 * width), whole((8, d))]
            + [whole((d, width))] * 2 + [whole((width, d))] * 2,
            out_specs=[rows_of(block, d)] * 3 + [rows_of(block, 2 * width), rows_of(block, d), whole((8, d)), whole((8, width))]),
        out_shape=[jax.ShapeDtypeStruct((rows, d), BF16), jax.ShapeDtypeStruct((rows, d), BF16), jax.ShapeDtypeStruct((rows, d), F32),
                   jax.ShapeDtypeStruct((rows, 2 * width), BF16), jax.ShapeDtypeStruct((rows, d), BF16),
                   jax.ShapeDtypeStruct((8, d), F32), jax.ShapeDtypeStruct((8, width), F32)],
        name=f"ffn_bwd_{half}",
        cost_estimate=pl.CostEstimate(flops=8 * rows * d * width, bytes_accessed=rows * (20 * d + 8 * width), transcendentals=0),
    )(core, pre, p_own, p_far, grad_out, slope, vecs, *ups, *downs)

def attn_norm_bwd_kernel(pre, d_pre, p_own, p_far, gain, w_own, w_other, dx_out, low, g_own, g_other, sums):
    n, inv = standardized(pre[...])
    g = d_pre[...] + (p_own[...].astype(F32) + p_far[...].astype(F32))
    dx = norm_back(n, inv, g * gain[...])
    dx_out[...] = dx
    dl = dx.astype(BF16)
    low[...] = dl
    g_own[...] = nt(dl, w_own[...]).astype(BF16)
    g_other[...] = nt(dl, w_other[...]).astype(BF16)
    stack = jnp.concatenate([col_sum(g * n), col_sum(g), col_sum(dx), jnp.zeros((5, dx.shape[1]), F32)], axis=0)
    @pl.when(pl.program_id(0) == 0)
    def _():
        sums[...] = stack
    @pl.when(pl.program_id(0) > 0)
    def _():
        sums[...] += stack

def attn_norm_bwd(pre, d_pre, p_own, p_far, gain, w_own, w_other, block=256):
    rows, d = pre.shape
    cols = w_own.shape[0]
    return pl.pallas_call(
        attn_norm_bwd_kernel, grid=(rows // block,),
        in_specs=[rows_of(block, d)] * 4 + [whole((1, d))] + [whole((cols, d))] * 2,
        out_specs=[rows_of(block, d)] * 2 + [rows_of(block, cols)] * 2 + [whole((8, d))],
        out_shape=[jax.ShapeDtypeStruct((rows, d), F32), jax.ShapeDtypeStruct((rows, d), BF16)]
        + [jax.ShapeDtypeStruct((rows, cols), BF16)] * 2 + [jax.ShapeDtypeStruct((8, d), F32)],
        name="attn_norm_bwd",
        cost_estimate=pl.CostEstimate(flops=4 * rows * d * cols, bytes_accessed=18 * rows * d, transcendentals=0),
    )(pre, d_pre, p_own, p_far, gain, w_own, w_other)

QB_F, KB_F, QB_B, KB_B = 256, 512, 256, 256

def swaps(bit):
    return [(i, i ^ bit) for i in range(lax.axis_size("dp"))]

def sum_dp(x):
    index = lax.axis_index("dp")
    bits = [1 << b for b in range(lax.axis_size("dp").bit_length() - 1)]
    for bit in bits:
        rows = x.shape[0] // 2
        side = (index // bit) % 2
        mine = lax.dynamic_slice_in_dim(x, side * rows, rows, 0)
        other = lax.dynamic_slice_in_dim(x, (1 - side) * rows, rows, 0)
        other = lax.ppermute(other, "dp", swaps(bit))
        x = (mine.astype(F32) + other.astype(F32)).astype(BF16)
    for bit in reversed(bits):
        side = (index // bit) % 2
        other = lax.ppermute(x, "dp", swaps(bit))
        x = jnp.where(side == 0, jnp.concatenate([x, other]), jnp.concatenate([other, x]))
    return x

def sum_dp_small(x):
    for b in range(lax.axis_size("dp").bit_length() - 1):
        x = x + lax.ppermute(x, "dp", swaps(1 << b))
    return x

def per_device(tokens, w_query, w_key, w_value, b_query, b_value, w_out, b_out, gain_attn, shift_attn,
               w_up, b_up, w_down, b_down, gain_ffn, shift_ffn, starts, grad_out):
    length, d = tokens.shape
    cols = w_query.shape[1]
    width = w_up.shape[1]
    quarter = length // 4
    tensor = lax.axis_index("tensor")
    core = tensor % 2
    core1 = core[None].astype(jnp.int32)
    far = tensor // 2
    group = lax.axis_size("tensor")
    swap_core = [(i, i ^ 1) for i in range(group)]
    swap_far = [(i, i ^ 2) for i in range(group)]

    def sib(x):
        return lax.ppermute(x, "tensor", swap_core)

    def across(x):
        return lax.ppermute(x, "tensor", swap_far)

    w_out_s, w_up_s, b_up_s, w_down_s = sib(w_out), sib(w_up), sib(b_up), sib(w_down)
    wqkv = jnp.concatenate([w_query, w_key, w_value], axis=1)
    wqkv_s = sib(wqkv)
    ups, downs, bus = (w_up, w_up_s), (w_down, w_down_s), (b_up[None], b_up_s[None])

    lim = limits(starts[0], length)
    count_f, count_b = counts(lim, QB_F, KB_F), counts(lim, QB_B, KB_B)
    lim = lim[None]
    q, k, v = project_qkv(tokens, w_query, w_key, w_value, b_query, b_value)
    vecs = jnp.stack([gain_attn, shift_attn, b_down, gain_ffn, shift_ffn] + [shift_ffn] * 3)

    mixed, attn, halves = [None] * 2, [None] * 2, [None] * 2
    for half in (0, 1):
        o, o32, lse = attn_fwd(half, count_f, q, k, v, lim, QB_F, KB_F)
        mine = lax.dynamic_slice_in_dim(o, core * quarter, quarter, 1)
        other = sib(lax.dynamic_slice_in_dim(o, (1 - core) * quarter, quarter, 1))
        mixed[half] = (mine, other)
        part = out_project(mine, other, w_out, w_out_s)
        attn[half] = (o32, lse)
        halves[half] = [part, across(part)]
    fwd = [None] * 2
    for half in (0, 1):
        fwd[half] = ffn_fwd(half, core1, tokens, *halves[half], b_out[None], gain_attn[None], shift_attn[None], ups, bus, downs)
        halves[half] = [fwd[half][4], across(fwd[half][4])]
    bwd = [None] * 2
    for half in (0, 1):
        bwd[half] = ffn_bwd(half, core1, fwd[half][0], *halves[half], grad_out, fwd[half][3], vecs, ups, downs)
        halves[half] = [bwd[half][4], across(bwd[half][4])]

    def over_rows(left, right):
        return tn(left[0], right[0]) + tn(left[1], right[1])

    act, d_low = [f[2] for f in fwd], [b[1] for b in bwd]
    low, d_up = [f[1] for f in fwd], [b[3] for b in bwd]
    down_other = sib(over_rows([a[:, width:] for a in act], d_low).astype(BF16))
    up_other = sib(over_rows(low, [u[:, width:] for u in d_up]).astype(BF16))
    g_down = over_rows([a[:, :width] for a in act], d_low) + down_other.astype(F32)
    g_up = over_rows(low, [u[:, :width] for u in d_up]) + up_other.astype(F32)
    g_down = sum_dp(g_down.astype(BF16))
    g_up = sum_dp(g_up.astype(BF16))

    res_own = [b[0] for b in bwd]
    res_sib = [sib(r) for r in res_own]
    pieces = []
    for half in (0, 1):
        pieces += [jnp.where(core == 0, res_own[half], res_sib[half]), jnp.where(core == 0, res_sib[half], res_own[half])]
    result = jnp.concatenate(pieces, axis=0)

    nb, grads = [None] * 2, [None] * 2
    carry, dqs = None, [None] * 2
    for half in (1, 0):
        nb[half] = attn_norm_bwd(fwd[half][0], bwd[half][2], *halves[half], gain_attn[None], w_out, w_out_s)
    for half in (1, 0):
        g_own, g_other = nb[half][2], sib(nb[half][3])
        g = jnp.where(core == 0, jnp.concatenate([g_own, g_other]), jnp.concatenate([g_other, g_own]))
        dq, dk, dv = attn_bwd(half, count_b, q, k, v, lim, attn[half][1], attn[half][0], g, carry, QB_B, KB_B)
        dqs[half] = dq
        carry = (dk, dv)
    d_all = jnp.concatenate([jnp.concatenate(dqs), carry[0].astype(BF16), carry[1].astype(BF16)], axis=1)

    a_low = [x[1] for x in nb]
    out_other = sib((nn(mixed[0][1], a_low[0]) + nn(mixed[1][1], a_low[1])).astype(BF16))
    g_out = nn(mixed[0][0], a_low[0]) + nn(mixed[1][0], a_low[1]) + out_other.astype(F32)
    g_out = sum_dp(g_out.astype(BF16))

    g_qkv = sum_dp(tn(tokens, d_all).astype(BF16))
    bias = jnp.sum(d_all.astype(F32), axis=0)
    ffn_sums = bwd[0][5] + bwd[1][5]
    attn_sums = nb[0][4] + nb[1][4]
    bup = bwd[0][6] + bwd[1][6]
    small = jnp.concatenate([attn_sums[:3], ffn_sums[:3]])
    small = small + sib(small)
    g_bup = bup[0] + sib(bup[1])
    packed = jnp.concatenate([small.reshape(-1), g_bup, bias])
    packed = sum_dp_small(packed)
    small = packed[:6 * d].reshape(6, d)
    g_bup = packed[6 * d:6 * d + width]
    bias = packed[6 * d + width:]

    d_quarters = d_all.reshape(4, quarter, 3 * cols)
    def quarter_of(i):
        return lax.dynamic_index_in_dim(d_quarters, i, 0, keepdims=False)
    def token_grad(h):
        return nt(quarter_of(2 * h + core), wqkv) + nt(sib(quarter_of(2 * h + 1 - core)), wqkv_s)
    sent = across(token_grad(1 - far).astype(BF16))
    grad_tokens = token_grad(far) + sent.astype(F32) + jnp.where(far == 0, nb[0][0], nb[1][0])
    return (result, grad_tokens, g_qkv[:, :cols].astype(F32), g_qkv[:, cols:2 * cols].astype(F32), g_qkv[:, 2 * cols:].astype(F32),
            bias[:cols], bias[2 * cols:], g_out.astype(F32), small[2], small[0], small[1],
            g_up.astype(F32), g_bup, g_down.astype(F32), small[5], small[3], small[4])

def solution(mesh):
    placed = (
        P("dp", None),
        P(None, "tensor"),
        P(None, "tensor"),
        P(None, "tensor"),
        P("tensor"),
        P("tensor"),
        P("tensor", None),
        P(),
        P(),
        P(),
        P(None, "tensor"),
        P("tensor"),
        P("tensor", None),
        P(),
        P(),
        P(),
        P("dp", None),
        P("dp", None),
    )
    return jax.shard_map(
        per_device,
        mesh=mesh,
        in_specs=placed,
        out_specs=(
            P("dp", None),
            P(("dp", "tensor"), None),
            P(None, "tensor"),
            P(None, "tensor"),
            P(None, "tensor"),
            P("tensor"),
            P("tensor"),
            P("tensor", None),
            P(),
            P(),
            P(),
            P(None, "tensor"),
            P("tensor"),
            P("tensor", None),
            P(),
            P(),
            P(),
        ),
        check_vma=False,
    )
```

```python
import functools
import jax, jax.numpy as jnp
from jax import lax
from jax.sharding import PartitionSpec as P
from jax.experimental import pallas as pl
from jax.experimental.pallas import tpu as pltpu
F32, BF16 = jnp.float32, jnp.bfloat16
HD = 64
PIECE = 256
QB_F, KB_F, QB_B, KB_B = 512, 512, 512, 256

def whole(shape):
    return pl.BlockSpec(shape, lambda *a: (0,) * len(shape))
NEG = -1e30

def nn(a, b):
    return lax.dot_general(a, b, (((1,), (0,)), ((), ())), preferred_element_type=F32)

def flip(x):
    return x.astype(F32).T.astype(BF16)

def spread_rows(t, heads):
    out = []
    zero = jnp.zeros((HD, t.shape[1]), t.dtype)
    for h in range(heads):
        out.append(jnp.concatenate([t[g * HD:(g + 1) * HD] if g == h else zero for g in range(heads)], axis=0))
    return out

def spread_cols(t, heads):
    lane = lax.broadcasted_iota(jnp.int32, t.shape, 1)
    return [jnp.where((lane >= h * HD) & (lane < (h + 1) * HD), t, jnp.zeros_like(t)) for h in range(heads)]

def row_limits(starts_ref, pieces, first, size, block):
    pos = lax.broadcasted_iota(jnp.int32, (1, size), 1) + first
    lim, last = pos, first + size - 1
    top = last
    for p in range(pieces):
        b = starts_ref[p]
        lim = jnp.where((pos >= b) & (pos < b + PIECE), b + PIECE - 1, lim)
        top = jnp.where((b <= last) & (b + PIECE > first), jnp.maximum(top, b + PIECE - 1), top)
    return lim, top // block + 1

def attn_fwd_kernel(half, pieces, QB, KB, starts_ref, q_ref, k_ref, vx, o_ref, o32_ref, lse_ref, acc, mx):
    rows = q_ref.shape[1]
    heads = q_ref.shape[0] // HD
    def q_block(i, c):
        qs = pl.ds(pl.multiple_of(i * QB, QB), QB)
        first = half * rows + i * QB
        lim, count = row_limits(starts_ref, pieces, first, QB, KB)
        qm = spread_rows(q_ref[:, qs], heads)
        acc[...] = jnp.zeros_like(acc)
        mx[...] = jnp.full_like(mx, NEG)
        def k_block(masked, j, c):
            ks = pl.ds(pl.multiple_of(j * KB, KB), KB)
            kk = k_ref[ks, :]
            if masked:
                ok = lax.broadcasted_iota(jnp.int32, (KB, QB), 0) + j * KB <= lim
            for h in range(heads):
                s = nn(kk, qm[h])
                if masked:
                    s = jnp.where(ok, s, NEG)
                old = mx[h]
                new = jnp.maximum(old, jnp.max(s, axis=0, keepdims=True))
                p = jnp.exp(s - new).astype(BF16)
                acc[h] = acc[h] * jnp.exp(old - new) + nn(vx[h, :, ks], p)
                mx[h] = new
            return c
        n_full = (first + 1) // KB
        lax.fori_loop(0, n_full, functools.partial(k_block, False), 0)
        lax.fori_loop(n_full, count, functools.partial(k_block, True), 0)
        for h in range(heads):
            a = acc[h]
            total = a[HD:HD + 1]
            o = a[:HD] / total
            o32_ref[h * HD:(h + 1) * HD, qs] = o
            o_ref[h * HD:(h + 1) * HD, qs] = o.astype(BF16)
            lse_ref[h:h + 1, qs] = mx[h] + jnp.log(total)
        return c
    lax.fori_loop(0, rows // QB, q_block, 0)

def attn_fwd(half, starts, qt, k, vx):
    QB, KB = QB_F, KB_F
    length, cols = k.shape
    heads = cols // HD
    rows = length // 2
    return pl.pallas_call(
        functools.partial(attn_fwd_kernel, half, starts.shape[0], QB, KB),
        grid_spec=pltpu.PrefetchScalarGridSpec(
            num_scalar_prefetch=1, grid=(1,),
            in_specs=[pl.BlockSpec((cols, rows), lambda i, c: (0, half)), whole((length, cols)), whole(vx.shape)],
            out_specs=[whole((cols, rows))] * 2 + [whole((heads, rows))],
            scratch_shapes=[pltpu.VMEM((heads, HD + 16, QB), F32), pltpu.VMEM((heads, 1, QB), F32)]),
        out_shape=[jax.ShapeDtypeStruct((cols, rows), BF16), jax.ShapeDtypeStruct((cols, rows), F32), jax.ShapeDtypeStruct((heads, rows), F32)],
        name=f"attn_fwd_{half}",
        cost_estimate=pl.CostEstimate(flops=(1 + 2 * half) * 4 * rows * rows * cols, bytes_accessed=6 * length * cols, transcendentals=rows * rows * heads),
    )(starts, qt, k, vx)

def attn_bwd_kernel(half, last, pieces, QB, KB, starts_ref, qt_ref, q_ref, k_ref, v_ref, kt, lse_ref, o32_ref, ga_ref, gb_ref, core_ref, *rest):
    if last:
        dk_in, dv_in, b_in, dq_ref, dk_out, dv_out, bias, dk_ref, dv_ref, dqt = rest[-10:]
    else:
        dq_ref, dk_ref, dv_ref, bias, dqt = rest[-5:]
    rows = q_ref.shape[0]
    heads = q_ref.shape[1] // HD
    length = k_ref.shape[0]
    if last:
        dk_ref[...] = dk_in[...]
        dv_ref[...] = dv_in[...]
        bias[...] = b_in[...]
    else:
        dk_ref[...] = jnp.zeros_like(dk_ref)
        dv_ref[...] = jnp.zeros_like(dv_ref)
        bias[...] = jnp.zeros_like(bias)
    share = ga_ref.shape[0]
    def q_block(i, c):
        qs = pl.ds(pl.multiple_of(i * QB, QB), QB)
        q = q_ref[qs, :]
        gs = pl.ds(pl.multiple_of(i * QB % share, QB), QB)
        g = jnp.where(i * QB // share == core_ref[0], ga_ref[gs, :], gb_ref[gs, :])
        gt32 = g.astype(F32).T
        qm = spread_rows(qt_ref[:, qs], heads)
        gm = spread_rows(gt32.astype(BF16), heads)
        qc = spread_cols(q, heads)
        gc = spread_cols(g, heads)
        prod = gt32 * o32_ref[:, qs]
        delta = [jnp.sum(prod[h * HD:(h + 1) * HD], axis=0, keepdims=True) for h in range(heads)]
        lse = [lse_ref[h:h + 1, qs] for h in range(heads)]
        first = half * rows + i * QB
        lim, count = row_limits(starts_ref, pieces, first, QB, KB)
        dqt[...] = jnp.zeros_like(dqt)
        def k_block(masked, j, c):
            ks = pl.ds(pl.multiple_of(j * KB, KB), KB)
            kk = k_ref[ks, :]
            vv = v_ref[ks, :]
            if masked:
                ok = lax.broadcasted_iota(jnp.int32, (KB, QB), 0) + j * KB <= lim
            dk = dk_ref[ks, :]
            dv = dv_ref[ks, :]
            for h in range(heads):
                s = nn(kk, qm[h])
                p = jnp.exp(s - lse[h])
                if masked:
                    p = jnp.where(ok, p, 0.0)
                dp = nn(vv, gm[h])
                ds = (p * (dp - delta[h])).astype(BF16)
                dv = dv + nn(p.astype(BF16), gc[h])
                dk = dk + nn(ds, qc[h])
                dqt[h * HD:(h + 1) * HD] += nn(kt[h * HD:(h + 1) * HD, ks], ds)
            dk_ref[ks, :] = dk
            dv_ref[ks, :] = dv
            return c
        n_full = (first + 1) // KB
        lax.fori_loop(0, n_full, functools.partial(k_block, False), 0)
        lax.fori_loop(n_full, count, functools.partial(k_block, True), 0)
        dq = (dqt[...] * 0.125).T.astype(BF16)
        dq_ref[qs, :] = dq
        bias[0:1] += jnp.sum(dq.astype(F32), axis=0, keepdims=True)
        return c
    lax.fori_loop(0, rows // QB, q_block, 0)
    if last:
        def finish(b, c):
            sl = pl.ds(pl.multiple_of(b * 256, 256), 256)
            dk_out[sl, :] = dk_ref[sl, :].astype(BF16)
            dv = dv_ref[sl, :].astype(BF16)
            dv_out[sl, :] = dv
            bias[1:2] += jnp.sum(dv.astype(F32), axis=0, keepdims=True)
            return c
        lax.fori_loop(0, length // 256, finish, 0)

def attn_bwd(half, starts, core, qt, q, k, v, kt, lse, o32, ga, gb, carry=None, deps=()):
    QB, KB = QB_B, KB_B
    length, cols = q.shape
    heads = cols // HD
    rows = length // 2
    last = carry is not None
    full = whole((length, cols))
    ins = [qt, q, k, v, kt, lse, o32, ga, gb, core] + list(deps)
    in_specs = [pl.BlockSpec((cols, rows), lambda i, c: (0, half)), pl.BlockSpec((rows, cols), lambda i, c: (half, 0)), full, full, whole((cols, length)),
                whole((heads, rows)), whole((cols, rows)), whole(ga.shape), whole(gb.shape), pl.BlockSpec(memory_space=pltpu.SMEM)]
    in_specs += [pl.BlockSpec(memory_space=pl.ANY)] * len(deps)
    if last:
        ins += list(carry)
        in_specs += [full, full, whole((8, cols))]
    kind = BF16 if last else F32
    return pl.pallas_call(
        functools.partial(attn_bwd_kernel, half, last, starts.shape[0], QB, KB),
        grid_spec=pltpu.PrefetchScalarGridSpec(
            num_scalar_prefetch=1, grid=(1,), in_specs=in_specs,
            out_specs=[whole((rows, cols)), full, full, whole((8, cols))],
            scratch_shapes=([pltpu.VMEM((length, cols), F32)] * 2 if last else []) + [pltpu.VMEM((cols, QB), F32)]),
        out_shape=[jax.ShapeDtypeStruct((rows, cols), BF16), jax.ShapeDtypeStruct((length, cols), kind), jax.ShapeDtypeStruct((length, cols), kind),
                   jax.ShapeDtypeStruct((8, cols), F32)],
        name=f"attn_bwd_{half}",
        cost_estimate=pl.CostEstimate(flops=(1 + 2 * half) * 10 * rows * rows * cols, bytes_accessed=20 * length * cols, transcendentals=rows * rows * heads),
    )(starts, *ins)

EPSILON = 1e-12

def nt(a, b):
    return lax.dot_general(a, b, (((1,), (1,)), ((), ())), preferred_element_type=F32)

def tn(a, b):
    return lax.dot_general(a, b, (((0,), (0,)), ((), ())), preferred_element_type=F32)

def standardized(v):
    spread = v - jnp.mean(v, axis=-1, keepdims=True)
    inv = lax.rsqrt(jnp.mean(spread * spread, axis=-1, keepdims=True) + EPSILON)
    return spread * inv, inv

def norm_back(n, inv, c):
    return inv * (c - jnp.mean(c, axis=-1, keepdims=True) - n * jnp.mean(c * n, axis=-1, keepdims=True))

def gelu_pair(v):
    cdf = 0.5 * (1.0 + lax.erf(v * 0.7071067811865476))
    pdf = jnp.exp(v * v * -0.5) * 0.3989422804014327
    return v * cdf, cdf + v * pdf

def qkv_kernel(tok, wq, wk, wv, bq, bv, q, k, v, qt, kt, vx):
    t = tok[...]
    a = ((nn(t, wq[...]) + bq[...]) * 0.125).astype(BF16)
    q[...] = a
    qt[...] = flip(a)
    a = nn(t, wk[...]).astype(BF16)
    k[...] = a
    kt[...] = flip(a)
    a = (nn(t, wv[...]) + bv[...]).astype(BF16)
    v[...] = a
    a = flip(a)
    one = jnp.where(lax.broadcasted_iota(jnp.int32, (16, a.shape[1]), 0) == 0, 1.0, 0.0).astype(BF16)
    for h in range(vx.shape[0]):
        vx[h] = jnp.concatenate([a[h * HD:(h + 1) * HD], one], axis=0)

def rows_of(block, cols):
    return pl.BlockSpec((block, cols), lambda i, *a: (i, 0))

def project_qkv(tokens, wq, wk, wv, bq, bv, block=512):
    rows, d = tokens.shape
    cols = wq.shape[1]
    return pl.pallas_call(
        qkv_kernel, grid=(rows // block,),
        in_specs=[rows_of(block, d)] + [whole((d, cols))] * 3 + [whole((1, cols))] * 2,
        out_specs=[rows_of(block, cols)] * 3 + [pl.BlockSpec((cols, block), lambda i: (0, i))] * 2 + [pl.BlockSpec((cols // HD, HD + 16, block), lambda i: (0, 0, i))],
        out_shape=[jax.ShapeDtypeStruct((rows, cols), BF16)] * 3 + [jax.ShapeDtypeStruct((cols, rows), BF16)] * 2
        + [jax.ShapeDtypeStruct((cols // HD, HD + 16, rows), BF16)],
        name="project_qkv",
        cost_estimate=pl.CostEstimate(flops=6 * rows * d * cols, bytes_accessed=2 * rows * (d + 3 * cols), transcendentals=0),
    )(tokens, wq, wk, wv, bq[None], bv[None])

def out_kernel(core, own, other, w_own, w_other, out):
    out[...] = (tn(own[...], w_own[...]) + tn(other[...], w_other[...])).astype(BF16)

def out_project(core, own, other, w_own, w_other):
    cols, rows = other.shape
    d = w_own.shape[1]
    return pl.pallas_call(
        out_kernel,
        grid_spec=pltpu.PrefetchScalarGridSpec(
            num_scalar_prefetch=1, grid=(1,),
            in_specs=[pl.BlockSpec((cols, rows), lambda i, c: (0, c[0])), whole((cols, rows)), whole((cols, d)), whole((cols, d))],
            out_specs=whole((rows, d))),
        out_shape=jax.ShapeDtypeStruct((rows, d), BF16), name="out_project",
        cost_estimate=pl.CostEstimate(flops=4 * rows * d * cols, bytes_accessed=2 * rows * (d + 2 * cols), transcendentals=0),
    )(core, own, other, w_own, w_other)

def ffn_fwd_kernel(spot, tok, p_own, p_far, b_out, gain, shift, up_a, up_b, bu_a, bu_b, down_a, down_b,
                   pre, low, act, slope, part):
    x = tok[...].astype(F32) + (p_own[...].astype(F32) + p_far[...].astype(F32)) + b_out[...]
    pre[...] = x
    n, inv = standardized(x)
    h = (n * gain[...] + shift[...]).astype(BF16)
    low[...] = h
    d = x.shape[1]
    total = None
    for s, (wu, bu, wd) in enumerate(((up_a, bu_a, down_a), (up_b, bu_b, down_b))):
        width = wu.shape[1]
        a, da = gelu_pair(nn(h, wu[...]) + bu[...])
        a = a.astype(BF16)
        act[:, s * width:(s + 1) * width] = a
        slope[:, s * width:(s + 1) * width] = da.astype(BF16)
        y = nn(a, wd[...])
        total = y if total is None else total + y
    part[...] = total.astype(BF16)

def ffn_fwd(half, core, tokens, p_own, p_far, b_out, gain, shift, ups, bus, downs, block=256):
    rows, d = p_own.shape
    width = ups[0].shape[1]
    steps = rows // block
    vec = whole((1, d))
    return pl.pallas_call(
        ffn_fwd_kernel,
        grid_spec=pltpu.PrefetchScalarGridSpec(
            num_scalar_prefetch=1, grid=(steps,),
            in_specs=[pl.BlockSpec((block, d), lambda i, c: ((2 * half + c[0]) * steps + i, 0)), rows_of(block, d), rows_of(block, d), vec, vec, vec]
            + [whole((d, width))] * 2 + [whole((1, width))] * 2 + [whole((width, d))] * 2,
            out_specs=[rows_of(block, d)] * 2 + [rows_of(block, 2 * width)] * 2 + [rows_of(block, d)]),
        out_shape=[jax.ShapeDtypeStruct((rows, d), F32), jax.ShapeDtypeStruct((rows, d), BF16)]
        + [jax.ShapeDtypeStruct((rows, 2 * width), BF16)] * 2 + [jax.ShapeDtypeStruct((rows, d), BF16)],
        name=f"ffn_fwd_{half}",
        cost_estimate=pl.CostEstimate(flops=8 * rows * d * width, bytes_accessed=rows * (14 * d + 8 * width), transcendentals=4 * rows * width),
    )(core, tokens, p_own, p_far, b_out, gain, shift, *ups, *bus, *downs)

def col_sum(v):
    return jnp.sum(v, axis=0, keepdims=True)

def ffn_bwd_kernel(spot, pre, p_own, p_far, go, slope, vecs, up_a, up_b, down_a, down_b,
                   result, d_low, d_pre, d_up, part, sums, bup):
    gain, shift, b_down, gain2, shift2 = (vecs[r:r + 1] for r in range(5))
    n, inv = standardized(pre[...])
    x = n * gain + shift + (p_own[...].astype(F32) + p_far[...].astype(F32)) + b_down
    n, inv = standardized(x)
    result[...] = (n * gain2 + shift2).astype(BF16)
    g = go[...].astype(F32)
    dx = norm_back(n, inv, g * gain2)
    d_pre[...] = dx
    dl = dx.astype(BF16)
    d_low[...] = dl
    stack = jnp.concatenate([col_sum(g * n), col_sum(g), col_sum(dx), jnp.zeros((5, dx.shape[1]), F32)], axis=0)
    total = None
    bu = []
    for s, (wu, wd) in enumerate(((up_a, down_a), (up_b, down_b))):
        width = wu.shape[1]
        sl = slice(s * width, (s + 1) * width)
        du = (nt(dl, wd[...]) * slope[:, sl].astype(F32)).astype(BF16)
        d_up[:, sl] = du
        bu.append(col_sum(du.astype(F32)))
        y = nt(du, wu[...])
        total = y if total is None else total + y
    part[...] = total.astype(BF16)
    bu = jnp.concatenate(bu + [jnp.zeros((6, bu[0].shape[1]), F32)], axis=0)
    @pl.when(pl.program_id(0) == 0)
    def _():
        sums[...] = stack
        bup[...] = bu
    @pl.when(pl.program_id(0) > 0)
    def _():
        sums[...] += stack
        bup[...] += bu

def ffn_bwd(half, core, pre, p_own, p_far, grad_out, slope, vecs, ups, downs, block=256):
    rows, d = pre.shape
    width = ups[0].shape[1]
    steps = rows // block
    return pl.pallas_call(
        ffn_bwd_kernel,
        grid_spec=pltpu.PrefetchScalarGridSpec(
            num_scalar_prefetch=1, grid=(steps,),
            in_specs=[rows_of(block, d)] * 3 + [pl.BlockSpec((block, d), lambda i, c: ((2 * half + c[0]) * steps + i, 0)), rows_of(block, 2 * width), whole((8, d))]
            + [whole((d, width))] * 2 + [whole((width, d))] * 2,
            out_specs=[rows_of(block, d)] * 3 + [rows_of(block, 2 * width), rows_of(block, d), whole((8, d)), whole((8, width))]),
        out_shape=[jax.ShapeDtypeStruct((rows, d), BF16), jax.ShapeDtypeStruct((rows, d), BF16), jax.ShapeDtypeStruct((rows, d), F32),
                   jax.ShapeDtypeStruct((rows, 2 * width), BF16), jax.ShapeDtypeStruct((rows, d), BF16),
                   jax.ShapeDtypeStruct((8, d), F32), jax.ShapeDtypeStruct((8, width), F32)],
        name=f"ffn_bwd_{half}",
        cost_estimate=pl.CostEstimate(flops=8 * rows * d * width, bytes_accessed=rows * (20 * d + 8 * width), transcendentals=0),
    )(core, pre, p_own, p_far, grad_out, slope, vecs, *ups, *downs)

def attn_norm_bwd_kernel(pre, d_pre, p_own, p_far, gain, w_own, w_other, *rest):
    dx_out, low, g_own, g_other, sums = rest[-5:]
    n, inv = standardized(pre[...])
    g = d_pre[...] + (p_own[...].astype(F32) + p_far[...].astype(F32))
    dx = norm_back(n, inv, g * gain[...])
    dx_out[...] = dx
    dl = dx.astype(BF16)
    low[...] = dl
    g_own[...] = nt(dl, w_own[...]).astype(BF16)
    g_other[...] = nt(dl, w_other[...]).astype(BF16)
    stack = jnp.concatenate([col_sum(g * n), col_sum(g), col_sum(dx), jnp.zeros((5, dx.shape[1]), F32)], axis=0)
    @pl.when(pl.program_id(0) == 0)
    def _():
        sums[...] = stack
    @pl.when(pl.program_id(0) > 0)
    def _():
        sums[...] += stack

def attn_norm_bwd(pre, d_pre, p_own, p_far, gain, w_own, w_other, deps=(), block=256):
    rows, d = pre.shape
    cols = w_own.shape[0]
    return pl.pallas_call(
        attn_norm_bwd_kernel, grid=(rows // block,),
        in_specs=[rows_of(block, d)] * 4 + [whole((1, d))] + [whole((cols, d))] * 2 + [pl.BlockSpec(memory_space=pl.ANY)] * len(deps),
        out_specs=[rows_of(block, d)] * 2 + [rows_of(block, cols)] * 2 + [whole((8, d))],
        out_shape=[jax.ShapeDtypeStruct((rows, d), F32), jax.ShapeDtypeStruct((rows, d), BF16)]
        + [jax.ShapeDtypeStruct((rows, cols), BF16)] * 2 + [jax.ShapeDtypeStruct((8, d), F32)],
        name="attn_norm_bwd",
        cost_estimate=pl.CostEstimate(flops=4 * rows * d * cols, bytes_accessed=18 * rows * d, transcendentals=0),
    )(pre, d_pre, p_own, p_far, gain, w_own, w_other, *deps)

def hop_kernel(plan, n_in, side_ref, *refs):
    ins, outs = list(refs[:n_in]), list(refs[len(refs) - sum(2 if p[0] == "split" else 1 for p in plan):])
    for p in plan:
        a, b = ins.pop(0), ins.pop(0) if p[1] else None
        def take(at, size):
            sl = pl.ds(at, size)
            x = a[sl, :].astype(F32)
            return x if b is None else x + b[sl, :].astype(F32)
        if p[0] == "add":
            o = outs.pop(0)
            o[...] = take(0, o.shape[0]).astype(o.dtype)
            continue
        side = side_ref[p[2]]
        if p[0] == "split":
            keep, send = outs.pop(0), outs.pop(0)
            half = keep.shape[0]
            keep[...] = take(pl.multiple_of(side * half, half), half).astype(keep.dtype)
            send[...] = take(pl.multiple_of((1 - side) * half, half), half).astype(send.dtype)
        else:
            o = outs.pop(0)
            half = a.shape[0]
            o[pl.ds(pl.multiple_of(side * half, half), half), :] = a[...].astype(o.dtype)
            o[pl.ds(pl.multiple_of((1 - side) * half, half), half), :] = b[...].astype(o.dtype)

def hop(name, sides, items, deps=()):
    ins, plan, shapes = [], [], []
    for kind, a, b, bit, dtype in items:
        ins += [a] if b is None else [a, b]
        plan.append((kind, b is not None, bit))
        rows = a.shape[0] * 2 if kind == "join" else a.shape[0] // 2 if kind == "split" else a.shape[0]
        shapes += [jax.ShapeDtypeStruct((rows,) + a.shape[1:], dtype)] * (2 if kind == "split" else 1)
    return pl.pallas_call(
        functools.partial(hop_kernel, plan, len(ins)), grid=(1,),
        in_specs=[pl.BlockSpec(memory_space=pltpu.SMEM)] + [whole(x.shape) for x in ins] + [pl.BlockSpec(memory_space=pl.ANY)] * len(deps),
        out_specs=[whole(s.shape) for s in shapes], out_shape=shapes, name=name,
        cost_estimate=pl.CostEstimate(flops=sum(x.size for x in ins), bytes_accessed=4 * sum(x.size for x in ins), transcendentals=0),
    )(sides, *ins, *deps)

def trade(x, bit):
    return lax.ppermute(x, "dp", [(i, i ^ (1 << bit)) for i in range(lax.axis_size("dp"))])

class DpSum:
    ORDERS = ((0, 1, 2), (1, 2, 0))

    def __init__(self, name, sides, pairs, small=None):
        self.name, self.sides, self.small, self.at = name, sides, small, 0
        items = [("split", a, b, order[0], BF16) for (a, b), order in zip(pairs, self.ORDERS)]
        self.cols = [[order[0], None] for order in self.ORDERS]
        self.launch(hop(name + "_0", sides, items))

    def launch(self, outs):
        self.keep, self.come = [], []
        for n, order in enumerate(self.ORDERS):
            keep, send = outs[2 * n:2 * n + 2]
            self.keep.append(keep)
            self.come.append(trade(send, order[self.at]))
        if self.small is not None:
            self.small_come = trade(self.small, self.at)

    def step(self, deps=(), dtype=BF16):
        self.at += 1
        at, name = self.at, f"{self.name}_{self.at}"
        if at <= 3:
            kind = "split" if at < 3 else "add"
            items = [(kind, k, c, o[at % 3], BF16) for k, c, o in zip(self.keep, self.come, self.ORDERS)]
            if self.small is not None:
                items.append(("add", self.small, self.small_come, None, F32))
            outs = hop(name, self.sides, items, deps)
            if self.small is not None:
                self.small = outs[-1]
            if at < 3:
                return self.launch(outs)
            self.keep = list(outs[:2])
            for bit in range(3, lax.axis_size("dp").bit_length() - 1):
                self.keep = [(k.astype(F32) + trade(k, bit).astype(F32)).astype(BF16) for k in self.keep]
                if self.small is not None:
                    self.small = self.small + trade(self.small, bit)
            self.come = [trade(k, o[2]) for k, o in zip(self.keep, self.ORDERS)]
        else:
            items = [("join", k, c, o[6 - at], dtype) for k, c, o in zip(self.keep, self.come, self.ORDERS)]
            self.keep = list(hop(name, self.sides, items, deps))
            if at < 6:
                self.come = [trade(k, o[5 - at]) for k, o in zip(self.keep, self.ORDERS)]
            return self.keep

ORDER = (1, 0)

def per_device(tokens, w_query, w_key, w_value, b_query, b_value, w_out, b_out, gain_attn, shift_attn,
               w_up, b_up, w_down, b_down, gain_ffn, shift_ffn, starts, grad_out):
    length, d = tokens.shape
    cols = w_query.shape[1]
    width = w_up.shape[1]
    quarter = length // 4
    tensor = lax.axis_index("tensor")
    core = tensor % 2
    core1 = core[None].astype(jnp.int32)
    far = tensor // 2
    group = lax.axis_size("tensor")
    swap_core = [(i, i ^ 1) for i in range(group)]
    swap_far = [(i, i ^ 2) for i in range(group)]

    def sib(x):
        return lax.ppermute(x, "tensor", swap_core)

    def across(x):
        return lax.ppermute(x, "tensor", swap_far)

    w_out_s, w_up_s, b_up_s, w_down_s = sib(w_out), sib(w_up), sib(b_up), sib(w_down)
    wqkv = jnp.concatenate([w_query, w_key, w_value], axis=1)
    wqkv_s = sib(wqkv)
    ups, downs, bus = (w_up, w_up_s), (w_down, w_down_s), (b_up[None], b_up_s[None])

    starts = starts[0]
    index = lax.axis_index("dp")
    sides = jnp.stack([(index >> b) % 2 for b in range(3)]).astype(jnp.int32)
    q, k, v, qt, kt, vx = project_qkv(tokens, w_query, w_key, w_value, b_query, b_value)
    vecs = jnp.stack([gain_attn, shift_attn, b_down, gain_ffn, shift_ffn] + [shift_ffn] * 3)

    mixed, attn, halves = [None] * 2, [None] * 2, [None] * 2
    for half in ORDER:
        o, o32, lse = attn_fwd(half, starts, qt, k, vx)
        other = sib(lax.dynamic_slice_in_dim(o, (1 - core) * quarter, quarter, 1))
        mixed[half] = (lax.dynamic_slice_in_dim(o, core * quarter, quarter, 1), other)
        part = out_project(core1, o, other, w_out, w_out_s)
        attn[half] = (o32, lse)
        halves[half] = [part, across(part)]
    fwd = [None] * 2
    for half in ORDER:
        fwd[half] = ffn_fwd(half, core1, tokens, *halves[half], b_out[None], gain_attn[None], shift_attn[None], ups, bus, downs)
        halves[half] = [fwd[half][4], across(fwd[half][4])]
    bwd = [None] * 2
    for half in ORDER:
        bwd[half] = ffn_bwd(half, core1, fwd[half][0], *halves[half], grad_out, fwd[half][3], vecs, ups, downs)
        halves[half] = [bwd[half][4], across(bwd[half][4])]

    def over_rows(left, right):
        return tn(left[0], right[0]) + tn(left[1], right[1])

    act, d_low = [f[2] for f in fwd], [b[1] for b in bwd]
    low, d_up = [f[1] for f in fwd], [b[3] for b in bwd]
    down_other = sib(over_rows([a[:, width:] for a in act], d_low).astype(BF16))
    up_other = sib(over_rows(low, [u[:, width:] for u in d_up]).astype(BF16))
    g_down = over_rows([a[:, :width] for a in act], d_low)
    g_up = over_rows(low, [u[:, :width] for u in d_up])
    ffn_sum = DpSum("ffn_grad", sides, [(g_down, down_other), (g_up, up_other)])

    res_own = [b[0] for b in bwd]
    res_sib = [sib(r) for r in res_own]
    pieces = []
    for half in (0, 1):
        pieces += [jnp.where(core == 0, res_own[half], res_sib[half]), jnp.where(core == 0, res_sib[half], res_own[half])]
    result = jnp.concatenate(pieces, axis=0)

    nb, dqs, carry = [None] * 2, [None] * 2, None
    for half in ORDER:
        deps = [] if carry is None else ffn_sum.keep
        nb[half] = attn_norm_bwd(fwd[half][0], bwd[half][2], *halves[half], gain_attn[None], w_out, w_out_s, deps)
        ffn_sum.step([nb[half][1]])
        dqs[half], *carry = attn_bwd(half, starts, core1, qt, q, k, v, kt, attn[half][1], attn[half][0],
                                     nb[half][2], sib(nb[half][3]), carry, ffn_sum.keep)
        ffn_sum.step([dqs[half]])
    dk, dv, bias = carry

    a_low = [x[1] for x in nb]
    def out_grad(m):
        return tn(a_low[0], m[0].T) + tn(a_low[1], m[1].T)
    out_other = sib(out_grad([m[1] for m in mixed]).astype(BF16))
    g_out = (out_grad([m[0] for m in mixed]) + out_other.astype(F32)).astype(BF16)

    half_rows = length // 2
    g_qkv = jnp.concatenate([(tn(tokens[:half_rows], dqs[0]) + tn(tokens[half_rows:], dqs[1])).astype(BF16),
                             tn(tokens, dk).astype(BF16), tn(tokens, dv).astype(BF16), g_out], axis=1)
    small = jnp.concatenate([(nb[0][4] + nb[1][4])[:3], (bwd[0][5] + bwd[1][5])[:3]])
    small = small + sib(small)
    bup = bwd[0][6] + bwd[1][6]
    g_bup = bup[0] + sib(bup[1])
    packed = jnp.concatenate([small.reshape(-1), g_bup, bias[0], bias[1]])
    packed = jnp.pad(packed, (0, -packed.shape[0] % 1024)).reshape(-1, 128)
    tail = DpSum("tail_grad", sides, [(g_qkv[:d // 2], None), (g_qkv[d // 2:], None)], packed)
    g_down, g_up = ffn_sum.step([tail.keep[0]])
    tail.step()
    g_down, g_up = ffn_sum.step([tail.keep[0]], F32)
    for _ in range(4):
        tail.step()
    g_qkv = jnp.concatenate(tail.step(dtype=F32))
    packed = tail.small.reshape(-1)
    small = packed[:6 * d].reshape(6, d)
    g_bup = packed[6 * d:6 * d + width]
    bias = packed[6 * d + width:]

    def quarter_of(i):
        rows = i % 2 * quarter
        dq = jnp.where(i < 2, lax.dynamic_slice_in_dim(dqs[0], rows, quarter, 0), lax.dynamic_slice_in_dim(dqs[1], rows, quarter, 0))
        return jnp.concatenate([dq] + [lax.dynamic_slice_in_dim(x, i * quarter, quarter, 0) for x in (dk, dv)], axis=1)
    def token_grad(h):
        return nt(quarter_of(2 * h + core), wqkv) + nt(sib(quarter_of(2 * h + 1 - core)), wqkv_s)
    sent = across(token_grad(1 - far).astype(BF16))
    grad_tokens = token_grad(far) + sent.astype(F32) + jnp.where(far == 0, nb[0][0], nb[1][0])
    return (result, grad_tokens, g_qkv[:, :cols], g_qkv[:, cols:2 * cols], g_qkv[:, 2 * cols:3 * cols],
            bias[:cols], bias[cols:2 * cols], g_qkv[:, 3 * cols:].T, small[2], small[0], small[1],
            g_up, g_bup, g_down, small[5], small[3], small[4])

def solution(mesh):
    placed = (
        P("dp", None),
        P(None, "tensor"),
        P(None, "tensor"),
        P(None, "tensor"),
        P("tensor"),
        P("tensor"),
        P("tensor", None),
        P(),
        P(),
        P(),
        P(None, "tensor"),
        P("tensor"),
        P("tensor", None),
        P(),
        P(),
        P(),
        P("dp", None),
        P("dp", None),
    )
    return jax.shard_map(
        per_device,
        mesh=mesh,
        in_specs=placed,
        out_specs=(
            P("dp", None),
            P(("dp", "tensor"), None),
            P(None, "tensor"),
            P(None, "tensor"),
            P(None, "tensor"),
            P("tensor"),
            P("tensor"),
            P("tensor", None),
            P(),
            P(),
            P(),
            P(None, "tensor"),
            P("tensor"),
            P("tensor", None),
            P(),
            P(),
            P(),
        ),
        check_vma=False,
    )
```

```python
import functools
import jax, jax.numpy as jnp
from jax import lax
from jax.sharding import PartitionSpec as P
from jax.experimental import pallas as pl
from jax.experimental.pallas import tpu as pltpu
F32, BF16 = jnp.float32, jnp.bfloat16
HD = 64
PIECE = 256
QB_F, KB_F, QB_B, KB_B = 512, 512, 512, 256

def whole(shape):
    return pl.BlockSpec(shape, lambda *a: (0,) * len(shape))
NEG = -1e30

def nn(a, b):
    return lax.dot_general(a, b, (((1,), (0,)), ((), ())), preferred_element_type=F32)

def flip(x):
    return x.astype(F32).T.astype(BF16)

def spread_rows(t, heads):
    out = []
    zero = jnp.zeros((HD, t.shape[1]), t.dtype)
    for h in range(heads):
        out.append(jnp.concatenate([t[g * HD:(g + 1) * HD] if g == h else zero for g in range(heads)], axis=0))
    return out

def spread_cols(t, heads):
    lane = lax.broadcasted_iota(jnp.int32, t.shape, 1)
    return [jnp.where((lane >= h * HD) & (lane < (h + 1) * HD), t, jnp.zeros_like(t)) for h in range(heads)]

def row_limits(starts_ref, pieces, first, size, block):
    pos = lax.broadcasted_iota(jnp.int32, (1, size), 1) + first
    lim, last = pos, first + size - 1
    top = last
    for p in range(pieces):
        b = starts_ref[p]
        lim = jnp.where((pos >= b) & (pos < b + PIECE), b + PIECE - 1, lim)
        top = jnp.where((b <= last) & (b + PIECE > first), jnp.maximum(top, b + PIECE - 1), top)
    return lim, top // block + 1

def attn_fwd_kernel(half, pieces, QB, KB, starts_ref, q_ref, k_ref, vx, o_ref, o32_ref, lse_ref, acc, mx):
    rows = q_ref.shape[1]
    heads = q_ref.shape[0] // HD
    def q_block(i, c):
        qs = pl.ds(pl.multiple_of(i * QB, QB), QB)
        first = half * rows + i * QB
        lim, count = row_limits(starts_ref, pieces, first, QB, KB)
        qm = spread_rows(q_ref[:, qs], heads)
        acc[...] = jnp.zeros_like(acc)
        mx[...] = jnp.full_like(mx, NEG)
        def k_block(masked, j, c):
            ks = pl.ds(pl.multiple_of(j * KB, KB), KB)
            kk = k_ref[ks, :]
            if masked:
                ok = lax.broadcasted_iota(jnp.int32, (KB, QB), 0) + j * KB <= lim
            for h in range(heads):
                s = nn(kk, qm[h])
                if masked:
                    s = jnp.where(ok, s, NEG)
                old = mx[h]
                new = jnp.maximum(old, jnp.max(s, axis=0, keepdims=True))
                p = jnp.exp(s - new).astype(BF16)
                acc[h] = acc[h] * jnp.exp(old - new) + nn(vx[h, :, ks], p)
                mx[h] = new
            return c
        n_full = (first + 1) // KB
        lax.fori_loop(0, n_full, functools.partial(k_block, False), 0)
        lax.fori_loop(n_full, count, functools.partial(k_block, True), 0)
        for h in range(heads):
            a = acc[h]
            total = a[HD:HD + 1]
            o = a[:HD] / total
            o32_ref[h * HD:(h + 1) * HD, qs] = o
            o_ref[h * HD:(h + 1) * HD, qs] = o.astype(BF16)
            lse_ref[h:h + 1, qs] = mx[h] + jnp.log(total)
        return c
    lax.fori_loop(0, rows // QB, q_block, 0)

def attn_fwd(half, starts, qt, k, vx):
    QB, KB = QB_F, KB_F
    length, cols = k.shape
    heads = cols // HD
    rows = length // 2
    return pl.pallas_call(
        functools.partial(attn_fwd_kernel, half, starts.shape[0], QB, KB),
        grid_spec=pltpu.PrefetchScalarGridSpec(
            num_scalar_prefetch=1, grid=(1,),
            in_specs=[pl.BlockSpec((cols, rows), lambda i, c: (0, half)), whole((length, cols)), whole(vx.shape)],
            out_specs=[whole((cols, rows))] * 2 + [whole((heads, rows))],
            scratch_shapes=[pltpu.VMEM((heads, HD + 16, QB), F32), pltpu.VMEM((heads, 1, QB), F32)]),
        out_shape=[jax.ShapeDtypeStruct((cols, rows), BF16), jax.ShapeDtypeStruct((cols, rows), F32), jax.ShapeDtypeStruct((heads, rows), F32)],
        name=f"attn_fwd_{half}",
        cost_estimate=pl.CostEstimate(flops=(1 + 2 * half) * 4 * rows * rows * cols, bytes_accessed=6 * length * cols, transcendentals=rows * rows * heads),
    )(starts, qt, k, vx)

def attn_bwd_kernel(first_row, begin, last, pieces, QB, KB, starts_ref, qt_ref, q_ref, k_ref, v_ref, kt, lse_ref, o32_ref, ga_ref, gb_ref, core_ref, *rest):
    rest = list(rest)
    dqt = rest.pop()
    rows = q_ref.shape[0]
    heads = q_ref.shape[1] // HD
    length = k_ref.shape[0]
    if last:
        dk_ref, dv_ref = rest[-2:]
        dq_ref, dk_out, dv_out = rest[-5:-2]
        dk_in, dv_in = rest[-7:-5]
    else:
        dq_ref, dk_ref, dv_ref = rest[-3:]
        dk_in, dv_in = rest[-5:-3] if not begin else (None, None)
    if begin:
        dk_ref[...] = jnp.zeros_like(dk_ref)
        dv_ref[...] = jnp.zeros_like(dv_ref)
    else:
        dk_ref[...] = dk_in[...]
        dv_ref[...] = dv_in[...]
    share = ga_ref.shape[0]
    def q_block(i, c):
        qs = pl.ds(pl.multiple_of(i * QB, QB), QB)
        q = q_ref[qs, :]
        gs = pl.ds(pl.multiple_of(i * QB % share, QB), QB)
        g = jnp.where((first_row + i * QB) // share % 2 == core_ref[0], ga_ref[gs, :], gb_ref[gs, :])
        gt32 = g.astype(F32).T
        qm = spread_rows(qt_ref[:, qs], heads)
        gm = spread_rows(gt32.astype(BF16), heads)
        qc = spread_cols(q, heads)
        gc = spread_cols(g, heads)
        prod = gt32 * o32_ref[:, qs]
        delta = [jnp.sum(prod[h * HD:(h + 1) * HD], axis=0, keepdims=True) for h in range(heads)]
        lse = [lse_ref[h:h + 1, qs] for h in range(heads)]
        first = first_row + i * QB
        lim, count = row_limits(starts_ref, pieces, first, QB, KB)
        dqt[...] = jnp.zeros_like(dqt)
        def k_block(masked, j, c):
            ks = pl.ds(pl.multiple_of(j * KB, KB), KB)
            kk = k_ref[ks, :]
            vv = v_ref[ks, :]
            if masked:
                ok = lax.broadcasted_iota(jnp.int32, (KB, QB), 0) + j * KB <= lim
            dk = dk_ref[ks, :]
            dv = dv_ref[ks, :]
            for h in range(heads):
                s = nn(kk, qm[h])
                p = jnp.exp(s - lse[h])
                if masked:
                    p = jnp.where(ok, p, 0.0)
                dp = nn(vv, gm[h])
                ds = (p * (dp - delta[h])).astype(BF16)
                dv = dv + nn(p.astype(BF16), gc[h])
                dk = dk + nn(ds, qc[h])
                dqt[h * HD:(h + 1) * HD] += nn(kt[h * HD:(h + 1) * HD, ks], ds)
            dk_ref[ks, :] = dk
            dv_ref[ks, :] = dv
            return c
        n_full = (first + 1) // KB
        lax.fori_loop(0, n_full, functools.partial(k_block, False), 0)
        lax.fori_loop(n_full, count, functools.partial(k_block, True), 0)
        dq_ref[:, qs] = (dqt[...] * 0.125).astype(BF16)
        return c
    lax.fori_loop(0, rows // QB, q_block, 0)
    if last:
        def finish(b, c):
            sl = pl.ds(pl.multiple_of(b * 256, 256), 256)
            dk_out[:, sl] = dk_ref[sl, :].T.astype(BF16)
            dv_out[:, sl] = dv_ref[sl, :].T.astype(BF16)
            return c
        lax.fori_loop(0, length // 256, finish, 0)

def attn_bwd(first, rows, last, starts, core, qt, q, k, v, kt, lse, o32, ga, gb, carry=None, deps=()):
    QB, KB = QB_B, KB_B
    length, cols = q.shape
    heads = cols // HD
    begin = carry is None
    full = whole((length, cols))
    at, inner = first // rows, first % (length // 2) // rows
    ins = [qt, q, k, v, kt, lse, o32, ga, gb, core] + list(deps)
    in_specs = [pl.BlockSpec((cols, rows), lambda i, c: (0, at)), pl.BlockSpec((rows, cols), lambda i, c: (at, 0)), full, full, whole((cols, length)),
                pl.BlockSpec((heads, rows), lambda i, c: (0, inner)), pl.BlockSpec((cols, rows), lambda i, c: (0, inner)),
                whole(ga.shape), whole(gb.shape), pl.BlockSpec(memory_space=pltpu.SMEM)]
    in_specs += [pl.BlockSpec(memory_space=pl.ANY)] * len(deps)
    if not begin:
        ins += list(carry)
        in_specs += [full, full]
    out = jax.ShapeDtypeStruct((cols, length), BF16) if last else jax.ShapeDtypeStruct((length, cols), F32)
    flops = 10 * rows * (first + rows // 2) * cols
    return pl.pallas_call(
        functools.partial(attn_bwd_kernel, first, begin, last, starts.shape[0], QB, KB),
        grid_spec=pltpu.PrefetchScalarGridSpec(
            num_scalar_prefetch=1, grid=(1,), in_specs=in_specs,
            out_specs=[whole((cols, rows)), whole(out.shape), whole(out.shape)],
            scratch_shapes=([pltpu.VMEM((length, cols), F32)] * 2 if last else []) + [pltpu.VMEM((cols, QB), F32)]),
        out_shape=[jax.ShapeDtypeStruct((cols, rows), BF16), out, out],
        name=f"attn_bwd_{first}",
        cost_estimate=pl.CostEstimate(flops=flops, bytes_accessed=20 * length * cols, transcendentals=flops // 640),
    )(starts, *ins)

EPSILON = 1e-12

def nt(a, b):
    return lax.dot_general(a, b, (((1,), (1,)), ((), ())), preferred_element_type=F32)

def tn(a, b):
    return lax.dot_general(a, b, (((0,), (0,)), ((), ())), preferred_element_type=F32)

def standardized(v):
    spread = v - jnp.mean(v, axis=-1, keepdims=True)
    inv = lax.rsqrt(jnp.mean(spread * spread, axis=-1, keepdims=True) + EPSILON)
    return spread * inv, inv

def norm_back(n, inv, c):
    return inv * (c - jnp.mean(c, axis=-1, keepdims=True) - n * jnp.mean(c * n, axis=-1, keepdims=True))

def gelu_pair(v):
    cdf = 0.5 * (1.0 + lax.erf(v * 0.7071067811865476))
    pdf = jnp.exp(v * v * -0.5) * 0.3989422804014327
    return v * cdf, cdf + v * pdf

def qkv_kernel(tok, wq, wk, wv, bq, bv, q, k, v, qt, kt, vx):
    t = tok[...]
    a = ((nt(t, wq[...]) + bq[...]) * 0.125).astype(BF16)
    q[...] = a
    qt[...] = flip(a)
    a = nt(t, wk[...]).astype(BF16)
    k[...] = a
    kt[...] = flip(a)
    a = (nt(t, wv[...]) + bv[...]).astype(BF16)
    v[...] = a
    a = flip(a)
    one = jnp.where(lax.broadcasted_iota(jnp.int32, (16, a.shape[1]), 0) == 0, 1.0, 0.0).astype(BF16)
    for h in range(vx.shape[0]):
        vx[h] = jnp.concatenate([a[h * HD:(h + 1) * HD], one], axis=0)

def rows_of(block, cols):
    return pl.BlockSpec((block, cols), lambda i, *a: (i, 0))

def project_qkv(tokens, wq, wk, wv, bq, bv, block=512):
    rows, d = tokens.shape
    cols = wq.shape[0]
    return pl.pallas_call(
        qkv_kernel, grid=(rows // block,),
        in_specs=[rows_of(block, d)] + [whole((cols, d))] * 3 + [whole((1, cols))] * 2,
        out_specs=[rows_of(block, cols)] * 3 + [pl.BlockSpec((cols, block), lambda i: (0, i))] * 2 + [pl.BlockSpec((cols // HD, HD + 16, block), lambda i: (0, 0, i))],
        out_shape=[jax.ShapeDtypeStruct((rows, cols), BF16)] * 3 + [jax.ShapeDtypeStruct((cols, rows), BF16)] * 2
        + [jax.ShapeDtypeStruct((cols // HD, HD + 16, rows), BF16)],
        name="project_qkv",
        cost_estimate=pl.CostEstimate(flops=6 * rows * d * cols, bytes_accessed=2 * rows * (d + 3 * cols), transcendentals=0),
    )(tokens, wq, wk, wv, bq[None], bv[None])

def out_kernel(core, own, other, w_own, w_other, out):
    out[...] = (tn(own[...], w_own[...]) + tn(other[...], w_other[...])).astype(BF16)

def out_project(core, own, other, w_own, w_other):
    cols, rows = other.shape
    d = w_own.shape[1]
    return pl.pallas_call(
        out_kernel,
        grid_spec=pltpu.PrefetchScalarGridSpec(
            num_scalar_prefetch=1, grid=(1,),
            in_specs=[pl.BlockSpec((cols, rows), lambda i, c: (0, c[0])), whole((cols, rows)), whole((cols, d)), whole((cols, d))],
            out_specs=whole((rows, d))),
        out_shape=jax.ShapeDtypeStruct((rows, d), BF16), name="out_project",
        cost_estimate=pl.CostEstimate(flops=4 * rows * d * cols, bytes_accessed=2 * rows * (d + 2 * cols), transcendentals=0),
    )(core, own, other, w_own, w_other)

def ffn_fwd_kernel(spot, tok, p_own, p_far, b_out, gain, shift, up_a, up_b, bu_a, bu_b, down_a, down_b,
                   pre, low, act, slope, part):
    x = tok[...].astype(F32) + (p_own[...].astype(F32) + p_far[...].astype(F32)) + b_out[...]
    pre[...] = x
    n, inv = standardized(x)
    h = (n * gain[...] + shift[...]).astype(BF16)
    low[...] = h
    d = x.shape[1]
    total = None
    for s, (wu, bu, wd) in enumerate(((up_a, bu_a, down_a), (up_b, bu_b, down_b))):
        width = wu.shape[1]
        a, da = gelu_pair(nn(h, wu[...]) + bu[...])
        a = a.astype(BF16)
        act[:, s * width:(s + 1) * width] = a
        slope[:, s * width:(s + 1) * width] = da.astype(BF16)
        y = nn(a, wd[...])
        total = y if total is None else total + y
    part[...] = total.astype(BF16)

def ffn_fwd(half, core, tokens, p_own, p_far, b_out, gain, shift, ups, bus, downs, block=256):
    rows, d = p_own.shape
    width = ups[0].shape[1]
    steps = rows // block
    vec = whole((1, d))
    return pl.pallas_call(
        ffn_fwd_kernel,
        grid_spec=pltpu.PrefetchScalarGridSpec(
            num_scalar_prefetch=1, grid=(steps,),
            in_specs=[pl.BlockSpec((block, d), lambda i, c: ((2 * half + c[0]) * steps + i, 0)), rows_of(block, d), rows_of(block, d), vec, vec, vec]
            + [whole((d, width))] * 2 + [whole((1, width))] * 2 + [whole((width, d))] * 2,
            out_specs=[rows_of(block, d)] * 2 + [rows_of(block, 2 * width)] * 2 + [rows_of(block, d)]),
        out_shape=[jax.ShapeDtypeStruct((rows, d), F32), jax.ShapeDtypeStruct((rows, d), BF16)]
        + [jax.ShapeDtypeStruct((rows, 2 * width), BF16)] * 2 + [jax.ShapeDtypeStruct((rows, d), BF16)],
        name=f"ffn_fwd_{half}",
        cost_estimate=pl.CostEstimate(flops=8 * rows * d * width, bytes_accessed=rows * (14 * d + 8 * width), transcendentals=4 * rows * width),
    )(core, tokens, p_own, p_far, b_out, gain, shift, *ups, *bus, *downs)

def col_sum(v):
    return jnp.sum(v, axis=0, keepdims=True)

def ffn_bwd_kernel(spot, pre, p_own, p_far, go, slope, vecs, up_a, up_b, down_a, down_b,
                   result, d_low, d_pre, d_up, part, sums, bup):
    gain, shift, b_down, gain2, shift2 = (vecs[r:r + 1] for r in range(5))
    n, inv = standardized(pre[...])
    x = n * gain + shift + (p_own[...].astype(F32) + p_far[...].astype(F32)) + b_down
    n, inv = standardized(x)
    result[...] = (n * gain2 + shift2).astype(BF16)
    g = go[...].astype(F32)
    dx = norm_back(n, inv, g * gain2)
    d_pre[...] = dx
    dl = dx.astype(BF16)
    d_low[...] = dl
    stack = jnp.concatenate([col_sum(g * n), col_sum(g), col_sum(dx), jnp.zeros((5, dx.shape[1]), F32)], axis=0)
    total = None
    bu = []
    for s, (wu, wd) in enumerate(((up_a, down_a), (up_b, down_b))):
        width = wu.shape[1]
        sl = slice(s * width, (s + 1) * width)
        du = (nt(dl, wd[...]) * slope[:, sl].astype(F32)).astype(BF16)
        d_up[:, sl] = du
        bu.append(col_sum(du.astype(F32)))
        y = nt(du, wu[...])
        total = y if total is None else total + y
    part[...] = total.astype(BF16)
    bu = jnp.concatenate(bu + [jnp.zeros((6, bu[0].shape[1]), F32)], axis=0)
    @pl.when(pl.program_id(0) == 0)
    def _():
        sums[...] = stack
        bup[...] = bu
    @pl.when(pl.program_id(0) > 0)
    def _():
        sums[...] += stack
        bup[...] += bu

def ffn_bwd(half, core, pre, p_own, p_far, grad_out, slope, vecs, ups, downs, block=256):
    rows, d = pre.shape
    width = ups[0].shape[1]
    steps = rows // block
    return pl.pallas_call(
        ffn_bwd_kernel,
        grid_spec=pltpu.PrefetchScalarGridSpec(
            num_scalar_prefetch=1, grid=(steps,),
            in_specs=[rows_of(block, d)] * 3 + [pl.BlockSpec((block, d), lambda i, c: ((2 * half + c[0]) * steps + i, 0)), rows_of(block, 2 * width), whole((8, d))]
            + [whole((d, width))] * 2 + [whole((width, d))] * 2,
            out_specs=[rows_of(block, d)] * 3 + [rows_of(block, 2 * width), rows_of(block, d), whole((8, d)), whole((8, width))]),
        out_shape=[jax.ShapeDtypeStruct((rows, d), BF16), jax.ShapeDtypeStruct((rows, d), BF16), jax.ShapeDtypeStruct((rows, d), F32),
                   jax.ShapeDtypeStruct((rows, 2 * width), BF16), jax.ShapeDtypeStruct((rows, d), BF16),
                   jax.ShapeDtypeStruct((8, d), F32), jax.ShapeDtypeStruct((8, width), F32)],
        name=f"ffn_bwd_{half}",
        cost_estimate=pl.CostEstimate(flops=8 * rows * d * width, bytes_accessed=rows * (20 * d + 8 * width), transcendentals=0),
    )(core, pre, p_own, p_far, grad_out, slope, vecs, *ups, *downs)

def attn_norm_bwd_kernel(pre, d_pre, p_own, p_far, gain, w_own, w_other, *rest):
    dx_out, low, g_own, g_other, sums = rest[-5:]
    n, inv = standardized(pre[...])
    g = d_pre[...] + (p_own[...].astype(F32) + p_far[...].astype(F32))
    dx = norm_back(n, inv, g * gain[...])
    dx_out[...] = dx
    dl = dx.astype(BF16)
    low[...] = dl
    g_own[...] = nt(dl, w_own[...]).astype(BF16)
    g_other[...] = nt(dl, w_other[...]).astype(BF16)
    stack = jnp.concatenate([col_sum(g * n), col_sum(g), col_sum(dx), jnp.zeros((5, dx.shape[1]), F32)], axis=0)
    @pl.when(pl.program_id(0) == 0)
    def _():
        sums[...] = stack
    @pl.when(pl.program_id(0) > 0)
    def _():
        sums[...] += stack

def attn_norm_bwd(pre, d_pre, p_own, p_far, gain, w_own, w_other, deps=(), block=256):
    rows, d = pre.shape
    cols = w_own.shape[0]
    return pl.pallas_call(
        attn_norm_bwd_kernel, grid=(rows // block,),
        in_specs=[rows_of(block, d)] * 4 + [whole((1, d))] + [whole((cols, d))] * 2 + [pl.BlockSpec(memory_space=pl.ANY)] * len(deps),
        out_specs=[rows_of(block, d)] * 2 + [rows_of(block, cols)] * 2 + [whole((8, d))],
        out_shape=[jax.ShapeDtypeStruct((rows, d), F32), jax.ShapeDtypeStruct((rows, d), BF16)]
        + [jax.ShapeDtypeStruct((rows, cols), BF16)] * 2 + [jax.ShapeDtypeStruct((8, d), F32)],
        name="attn_norm_bwd",
        cost_estimate=pl.CostEstimate(flops=4 * rows * d * cols, bytes_accessed=18 * rows * d, transcendentals=0),
    )(pre, d_pre, p_own, p_far, gain, w_own, w_other, *deps)

def qkv_grad_kernel(side, dq0, dq1, dk, dv, tok, g_out, *rest):
    keep_a, send_a, keep_b, send_b, bias = rest[-5:]
    t = tok[...]
    half = dq0.shape[1]
    gq = (nn(dq0[...], tok[:half]) + nn(dq1[...], tok[half:])).astype(BF16)
    gk = nn(dk[...], t).astype(BF16)
    gv = nn(dv[...], t).astype(BF16)
    go = g_out[...]
    for s, keep, send, low, high in ((side[0], keep_a, send_a, gq, gk), (side[1], keep_b, send_b, gv, go)):
        @pl.when(s == 0)
        def _(keep=keep, send=send, low=low, high=high):
            keep[...] = low
            send[...] = high
        @pl.when(s != 0)
        def _(keep=keep, send=send, low=low, high=high):
            keep[...] = high
            send[...] = low
    one = jnp.ones((half, 128), BF16)
    cols = dk.shape[0]
    bias[:cols] = nn(dq0[...], one) + nn(dq1[...], one)
    bias[cols:] = nn(dv[:, :half], one) + nn(dv[:, half:], one)

def qkv_grad(sides, dq0, dq1, dk, dv, tokens, g_out, deps=()):
    cols, length = dk.shape
    d = tokens.shape[1]
    ins = [dq0, dq1, dk, dv, tokens, g_out]
    return pl.pallas_call(
        qkv_grad_kernel, grid=(1,),
        in_specs=[pl.BlockSpec(memory_space=pltpu.SMEM)] + [whole(x.shape) for x in ins] + [pl.BlockSpec(memory_space=pl.ANY)] * len(deps),
        out_specs=[whole((cols, d))] * 4 + [whole((2 * cols, 128))],
        out_shape=[jax.ShapeDtypeStruct((cols, d), BF16)] * 4 + [jax.ShapeDtypeStruct((2 * cols, 128), F32)],
        name="qkv_grad",
        cost_estimate=pl.CostEstimate(flops=6 * cols * length * d, bytes_accessed=2 * length * (d + 3 * cols), transcendentals=0),
    )(sides, *ins, *deps)

def hop_kernel(plan, n_in, side_ref, *refs):
    ins, outs = list(refs[:n_in]), list(refs[len(refs) - sum(2 if p[0] == "split" else 1 for p in plan):])
    for p in plan:
        a, b = ins.pop(0), ins.pop(0) if p[1] else None
        def take(at, size):
            sl = pl.ds(at, size)
            x = a[sl, :].astype(F32)
            return x if b is None else x + b[sl, :].astype(F32)
        if p[0] == "add":
            o = outs.pop(0)
            o[...] = take(0, o.shape[0]).astype(o.dtype)
            continue
        side = side_ref[p[2]]
        if p[0] == "split":
            keep, send = outs.pop(0), outs.pop(0)
            half = keep.shape[0]
            keep[...] = take(pl.multiple_of(side * half, half), half).astype(keep.dtype)
            send[...] = take(pl.multiple_of((1 - side) * half, half), half).astype(send.dtype)
        else:
            o = outs.pop(0)
            half = a.shape[0]
            o[pl.ds(pl.multiple_of(side * half, half), half), :] = a[...].astype(o.dtype)
            o[pl.ds(pl.multiple_of((1 - side) * half, half), half), :] = b[...].astype(o.dtype)

def hop(name, sides, items, deps=()):
    ins, plan, shapes = [], [], []
    for kind, a, b, bit, dtype in items:
        ins += [a] if b is None else [a, b]
        plan.append((kind, b is not None, bit))
        rows = a.shape[0] * 2 if kind == "join" else a.shape[0] // 2 if kind == "split" else a.shape[0]
        shapes += [jax.ShapeDtypeStruct((rows,) + a.shape[1:], dtype)] * (2 if kind == "split" else 1)
    return pl.pallas_call(
        functools.partial(hop_kernel, plan, len(ins)), grid=(1,),
        in_specs=[pl.BlockSpec(memory_space=pltpu.SMEM)] + [whole(x.shape) for x in ins] + [pl.BlockSpec(memory_space=pl.ANY)] * len(deps),
        out_specs=[whole(s.shape) for s in shapes], out_shape=shapes, name=name,
        cost_estimate=pl.CostEstimate(flops=sum(x.size for x in ins), bytes_accessed=4 * sum(x.size for x in ins), transcendentals=0),
    )(sides, *ins, *deps)

def trade(x, bit):
    return lax.ppermute(x, "dp", [(i, i ^ (1 << bit)) for i in range(lax.axis_size("dp"))])

class DpSum:
    ORDERS = ((0, 1, 2), (1, 2, 0))

    def __init__(self, name, sides, pairs, small=None, made=None, deps=()):
        self.name, self.sides, self.small, self.at = name, sides, small, 0
        if made is None:
            items = [("split", a, b, order[0], BF16) for (a, b), order in zip(pairs, self.ORDERS)]
            made = hop(name + "_0", sides, items, deps)
        self.launch(made)

    def launch(self, outs):
        self.keep, self.come = [], []
        for n, order in enumerate(self.ORDERS):
            keep, send = outs[2 * n:2 * n + 2]
            self.keep.append(keep)
            self.come.append(trade(send, order[self.at]))
        if self.small is not None:
            self.small_come = trade(self.small, self.at)

    def step(self, deps=(), dtype=BF16):
        self.at += 1
        at, name = self.at, f"{self.name}_{self.at}"
        if at <= 3:
            kind = "split" if at < 3 else "add"
            items = [(kind, k, c, o[at % 3], BF16) for k, c, o in zip(self.keep, self.come, self.ORDERS)]
            if self.small is not None:
                items.append(("add", self.small, self.small_come, None, F32))
            outs = hop(name, self.sides, items, deps)
            if self.small is not None:
                self.small = outs[-1]
            if at < 3:
                return self.launch(outs)
            self.keep = list(outs[:2])
            for bit in range(3, lax.axis_size("dp").bit_length() - 1):
                self.keep = [(k.astype(F32) + trade(k, bit).astype(F32)).astype(BF16) for k in self.keep]
                if self.small is not None:
                    self.small = self.small + trade(self.small, bit)
            self.come = [trade(k, o[2]) for k, o in zip(self.keep, self.ORDERS)]
        else:
            items = [("join", k, c, o[6 - at], dtype) for k, c, o in zip(self.keep, self.come, self.ORDERS)]
            self.keep = list(hop(name, self.sides, items, deps))
            if at < 6:
                self.come = [trade(k, o[5 - at]) for k, o in zip(self.keep, self.ORDERS)]
            return self.keep

ORDER = (1, 0)

def per_device(tokens, w_query, w_key, w_value, b_query, b_value, w_out, b_out, gain_attn, shift_attn,
               w_up, b_up, w_down, b_down, gain_ffn, shift_ffn, starts, grad_out):
    length, d = tokens.shape
    cols = w_query.shape[1]
    width = w_up.shape[1]
    quarter = length // 4
    tensor = lax.axis_index("tensor")
    core = tensor % 2
    core1 = core[None].astype(jnp.int32)
    far = tensor // 2
    group = lax.axis_size("tensor")
    swap_core = [(i, i ^ 1) for i in range(group)]
    swap_far = [(i, i ^ 2) for i in range(group)]

    def sib(x):
        return lax.ppermute(x, "tensor", swap_core)

    def across(x):
        return lax.ppermute(x, "tensor", swap_far)

    w_out_s, w_up_s, b_up_s, w_down_s = sib(w_out), sib(w_up), sib(b_up), sib(w_down)
    wqkv = jnp.concatenate([w_query.T, w_key.T, w_value.T])
    wqkv_s = sib(wqkv)
    ups, downs, bus = (w_up, w_up_s), (w_down, w_down_s), (b_up[None], b_up_s[None])

    starts = starts[0]
    index = lax.axis_index("dp")
    sides = jnp.stack([(index >> b) % 2 for b in range(3)]).astype(jnp.int32)
    q, k, v, qt, kt, vx = project_qkv(tokens, w_query.T, w_key.T, w_value.T, b_query, b_value)
    vecs = jnp.stack([gain_attn, shift_attn, b_down, gain_ffn, shift_ffn] + [shift_ffn] * 3)

    mixed, attn, halves = [None] * 2, [None] * 2, [None] * 2
    for half in ORDER:
        o, o32, lse = attn_fwd(half, starts, qt, k, vx)
        other = sib(lax.dynamic_slice_in_dim(o, (1 - core) * quarter, quarter, 1))
        mixed[half] = (lax.dynamic_slice_in_dim(o, core * quarter, quarter, 1), other)
        part = out_project(core1, o, other, w_out, w_out_s)
        attn[half] = (o32, lse)
        halves[half] = [part, across(part)]
    fwd = [None] * 2
    for half in ORDER:
        fwd[half] = ffn_fwd(half, core1, tokens, *halves[half], b_out[None], gain_attn[None], shift_attn[None], ups, bus, downs)
        halves[half] = [fwd[half][4], across(fwd[half][4])]
    bwd = [None] * 2
    for half in ORDER:
        bwd[half] = ffn_bwd(half, core1, fwd[half][0], *halves[half], grad_out, fwd[half][3], vecs, ups, downs)
        halves[half] = [bwd[half][4], across(bwd[half][4])]

    def over_rows(left, right):
        return tn(left[0], right[0]) + tn(left[1], right[1])

    act, d_low = [f[2] for f in fwd], [b[1] for b in bwd]
    low, d_up = [f[1] for f in fwd], [b[3] for b in bwd]
    down_other = sib(over_rows([a[:, width:] for a in act], d_low).astype(BF16))
    up_other = sib(over_rows(low, [u[:, width:] for u in d_up]).astype(BF16))
    g_down = over_rows([a[:, :width] for a in act], d_low)
    g_up = over_rows(low, [u[:, :width] for u in d_up])
    ffn_sum = DpSum("ffn_grad", sides, [(g_down, down_other), (g_up, up_other)])

    res_own = [b[0] for b in bwd]
    res_sib = [sib(r) for r in res_own]
    pieces = []
    for half in (0, 1):
        pieces += [jnp.where(core == 0, res_own[half], res_sib[half]), jnp.where(core == 0, res_sib[half], res_own[half])]
    result = jnp.concatenate(pieces, axis=0)

    half_rows = length // 2
    nb = [None] * 2

    def norm_back_of(half):
        nb[half] = attn_norm_bwd(fwd[half][0], bwd[half][2], *halves[half], gain_attn[None], w_out, w_out_s, ffn_sum.keep)
        ffn_sum.step([nb[half][1]])
        return nb[half][2], sib(nb[half][3])

    def attn_back(half, first, rows, last, g, carry):
        out = attn_bwd(first, rows, last, starts, core1, qt, q, k, v, kt, attn[half][1], attn[half][0], *g, carry, ffn_sum.keep)
        ffn_sum.step([out[0]])
        return out[0], out[1:]

    g = norm_back_of(1)
    dq1b, carry = attn_back(1, 3 * quarter, quarter, False, g, None)
    dq1a, carry = attn_back(1, 2 * quarter, quarter, False, g, carry)
    dq1 = jnp.concatenate([dq1a, dq1b], axis=1)
    g = norm_back_of(0)
    a_low = [x[1] for x in nb]
    def out_grad(m):
        return nn(m[0], a_low[0]) + nn(m[1], a_low[1])
    out_other = sib(out_grad([m[1] for m in mixed]).astype(BF16))
    g_out = (out_grad([m[0] for m in mixed]) + out_other.astype(F32)).astype(BF16)
    dq0, (dk, dv) = attn_back(0, 0, half_rows, True, g, carry)

    *made, bias = qkv_grad(sides, dq0, dq1, dk, dv, tokens, g_out, ffn_sum.keep)
    small = jnp.concatenate([(nb[0][4] + nb[1][4])[:3], (bwd[0][5] + bwd[1][5])[:3]])
    small = small + sib(small)
    bup = bwd[0][6] + bwd[1][6]
    g_bup = bup[0] + sib(bup[1])
    packed = jnp.concatenate([small.reshape(-1), g_bup, bias[:, 0]])
    packed = jnp.pad(packed, (0, -packed.shape[0] % 1024)).reshape(-1, 128)
    tail = DpSum("tail_grad", sides, None, packed, made)
    tail.step()
    tail.step()
    g_down, g_up = ffn_sum.step([tail.keep[0]], F32)
    for _ in range(3):
        tail.step()
    (g_q, g_k), (g_v, g_o) = ((x[:cols], x[cols:]) for x in tail.step(dtype=F32))
    packed = tail.small.reshape(-1)
    small = packed[:6 * d].reshape(6, d)
    g_bup = packed[6 * d:6 * d + width]
    bias = packed[6 * d + width:]

    dqs = [dq0[:, :quarter], dq0[:, quarter:], dq1a, dq1b]
    def quarter_of(h, c):
        low, high = (jnp.where(c == 0, dqs[2 * i], dqs[2 * i + 1]) for i in range(2))
        dq = jnp.where(h == 0, low, high)
        return jnp.concatenate([dq] + [lax.dynamic_slice_in_dim(x, (2 * h + c) * quarter, quarter, 1) for x in (dk, dv)])
    def token_grad(h):
        return tn(quarter_of(h, core), wqkv) + tn(sib(quarter_of(h, 1 - core)), wqkv_s)
    sent = across(token_grad(1 - far).astype(BF16))
    grad_tokens = token_grad(far) + sent.astype(F32) + jnp.where(far == 0, nb[0][0], nb[1][0])
    return (result, grad_tokens, g_q.T, g_k.T, g_v.T,
            bias[:cols], bias[cols:2 * cols], g_o, small[2], small[0], small[1],
            g_up, g_bup, g_down, small[5], small[3], small[4])

def solution(mesh):
    placed = (
        P("dp", None),
        P(None, "tensor"),
        P(None, "tensor"),
        P(None, "tensor"),
        P("tensor"),
        P("tensor"),
        P("tensor", None),
        P(),
        P(),
        P(),
        P(None, "tensor"),
        P("tensor"),
        P("tensor", None),
        P(),
        P(),
        P(),
        P("dp", None),
        P("dp", None),
    )
    return jax.shard_map(
        per_device,
        mesh=mesh,
        in_specs=placed,
        out_specs=(
            P("dp", None),
            P(("dp", "tensor"), None),
            P(None, "tensor"),
            P(None, "tensor"),
            P(None, "tensor"),
            P("tensor"),
            P("tensor"),
            P("tensor", None),
            P(),
            P(),
            P(),
            P(None, "tensor"),
            P("tensor"),
            P("tensor", None),
            P(),
            P(),
            P(),
        ),
        check_vma=False,
    )
```
